32 devices in a mesh: chan: 8 (over z, y), row: 2 (over core), col: 2 (over x).
Axes of the slice: x: 2, y: 2, z: 4, core: 2. Of those that a mesh axis runs over, the one named last changes fastest.
Arguments:
- volts: bfloat16 [2, 1024, 2, 52736], P(None, ('chan', 'row', 'col')), may hold values from -6 to 6
- taps: float32 [8, 512], replicated, may hold values from -2 to 2
- owner_map: int32 [24], replicated, may hold values from 0 to 15, as said below
- assign: int32 [512], replicated, may hold values from 0 to 511, each once
Outputs:
- visibility: bfloat16 [32, 2, 1024, 1024], P(('chan', 'col'), None, 'row')
The draws below stay inside these ranges and needn't reach their ends.
Inputs may be any that keep to these rules, and one draw needn't show every extreme that they name: `owner_map`: each owner holds 1 to 2 channels, and some owner holds exactly 2. `assign`: A permutation of the stations.
All inputs are finite; a program needn't handle non-finite values.
Results may differ from the reference program's by a relative error of at most 0.0055.
Values may be sent and summed in bfloat16 or wider, within the bound.
No kernel may reach another device: no remote copies, remote signals or barrier semaphores. Data moves between devices by JAX's collectives and lax.ppermute only.
A program may use at most 192 MiB of HBM per device.

```python
import math
import jax
import jax.numpy as jnp
from jax import lax

STATIONS = 512
NFFT = 512
TAPS = 8
BATCHES = 2
SPEC_B = 96
CAP = 2
INPUTS = 1024
SAMPLES = 52736
OWNERS = 16
NCHAN = 24


def draw_owner_map(key, part):
    pair_count = OWNERS // 2
    key_flips, key_owner, key_channel = jax.random.split(jax.random.fold_in(key, 7), 3)
    flips = jax.random.randint(key_flips, (pair_count,), 0, 2)
    sizes = jnp.stack([1 + flips * (CAP - 1), CAP - flips * (CAP - 1)], axis=1).reshape(OWNERS)
    sizes = jnp.take(sizes, jax.random.permutation(key_owner, OWNERS), axis=0)
    bounds = jnp.cumsum(sizes)
    places = jnp.arange(NCHAN)
    sorted_owner = jnp.sum((bounds[None, :] <= places[:, None]).astype(jnp.int32), axis=1)
    shuffle = jax.random.permutation(key_channel, NCHAN)
    return jnp.take(sorted_owner, shuffle, axis=0).astype(jnp.int32)


def shard_levels(rng, extent, cuts, low, top_value):
    loudness = 1.0
    for dim, parts in cuts:
        steps = jax.random.uniform(jax.random.fold_in(jax.random.fold_in(rng, 6), dim), (parts,), jnp.float32, low / len(cuts), top_value / len(cuts))
        loudness = loudness * jnp.repeat(jnp.exp(steps), extent[dim] // parts).reshape((-1,) + (1,) * (len(extent) - 1 - dim))
    return loudness


def centred(rng, extent, spread, most, cuts=(), kind=jnp.bfloat16):
    level = shard_levels(rng, extent, cuts, -0.22, 0.18) if cuts else 1.0
    entries = jax.random.normal(rng, extent, jnp.float32) * spread * level
    return jnp.minimum(jnp.maximum(entries, -most), most).astype(kind)


def setup_inputs(seed: int = 0) -> dict:
    seeds = jax.random.split(jax.random.key(seed), 5)
    volts = centred(seeds[0], (BATCHES, INPUTS, 2, SAMPLES), 1.0, 6.0, ((1, 32),))
    taps = centred(seeds[1], (TAPS, NFFT), TAPS ** -0.5, 2.0, (), jnp.float32)
    owner_map = draw_owner_map(jax.random.fold_in(seeds[4], 71), 0)
    assign = jax.random.permutation(seeds[3], STATIONS).astype(jnp.int32)
    return dict(volts=volts, taps=taps, owner_map=owner_map, assign=assign)


def slot_table(owner_map, owner_count, slot_count):
    channel_count = owner_map.shape[0]
    ranking = jnp.argsort(owner_map * channel_count + jnp.arange(channel_count, dtype=jnp.int32)).astype(jnp.int32)
    counts = lax.optimization_barrier(jnp.sum((owner_map[None, :] == jnp.arange(owner_count, dtype=jnp.int32)[:, None]).astype(jnp.int32), axis=1))
    starts = jnp.cumsum(counts) - counts
    slot_index = jnp.arange(slot_count, dtype=jnp.int32)
    position = jnp.clip(starts[:, None] + slot_index[None, :], 0, channel_count - 1).astype(jnp.int32)
    channel = jnp.take(ranking, position, axis=0)
    is_live = slot_index[None, :] < counts[:, None]
    return (channel, is_live)

def filter_bank(volts_batch, taps):
    count = volts_batch.shape[0]
    signal = volts_batch.astype(jnp.float32).reshape(count, 2, SPEC_B + TAPS - 1, NFFT)
    summed = jnp.zeros((count, 2, SPEC_B, NFFT), jnp.float32)
    for tap_index in range(TAPS):
        summed = summed + taps[tap_index][None, None, None, :] * signal[:, :, tap_index:tap_index + SPEC_B, :]
    return summed

def reference(volts, taps, owner_map, assign):
    points = jnp.arange(NFFT, dtype=jnp.int32)
    channels = jnp.arange(NCHAN, dtype=jnp.int32)
    phase = (points[:, None] * channels[None, :] % NFFT).astype(jnp.float32) * (2.0 * math.pi / NFFT)
    unit = 1.0 / math.sqrt(NFFT)
    cosine = jnp.cos(phase) * unit
    sine = jnp.sin(phase) * unit
    high = lax.Precision.HIGHEST
    spectra_list = []
    for batch in range(BATCHES):
        summed = filter_bank(volts[batch], taps)
        real_in = summed[:, 0]
        imag_in = summed[:, 1]
        real_out = jnp.einsum('isj,jk->iks', real_in, cosine, precision=high) + jnp.einsum('isj,jk->iks', imag_in, sine, precision=high)
        imag_out = jnp.einsum('isj,jk->iks', imag_in, cosine, precision=high) - jnp.einsum('isj,jk->iks', real_in, sine, precision=high)
        spectra_list.append(jnp.concatenate([real_out, imag_out], axis=2).astype(jnp.bfloat16))
    spectra = jnp.stack(spectra_list, 0)
    channel, is_live = slot_table(owner_map, OWNERS, CAP)
    positions = jnp.arange(INPUTS, dtype=jnp.int32)
    pick = (2 * jnp.take(assign, positions // 2, axis=0) + positions % 2).astype(jnp.int32)
    scale = 1.0 / math.sqrt(2 * BATCHES * SPEC_B)

    def one_slot(entry):
        slot_channel, slot_live = entry
        total = jnp.zeros((2 * INPUTS, INPUTS), jnp.float32)
        for batch in range(BATCHES):
            chosen = jnp.take(spectra[batch], slot_channel, axis=1)
            ordered = jnp.take(chosen, pick, axis=0)
            flipped = jnp.concatenate([ordered[:, SPEC_B:], -ordered[:, :SPEC_B]], axis=1)
            stacked = jnp.concatenate([ordered, flipped], axis=0)
            total = total + jnp.dot(stacked, ordered.T, preferred_element_type=jnp.float32)
        total = jnp.where(slot_live, total, jnp.zeros_like(total)) * scale
        return total.reshape(2, INPUTS, INPUTS).astype(jnp.bfloat16)
    return lax.map(one_slot, (channel.reshape(-1), is_live.reshape(-1)))
```

```python
import functools
import math

import jax
import jax.numpy as jnp
import numpy as np
from jax import lax
from jax.experimental import pallas as pl
from jax.experimental.pallas import tpu as pltpu
from jax.sharding import PartitionSpec as P

STATIONS = 512
NFFT = 512
TAPS = 8
BATCHES = 2
CAP = 2
LANES = 128


def slot_table(owner_map, owner_count, slot_count):
    channel_count = owner_map.shape[0]
    ranking = jnp.argsort(owner_map * channel_count + jnp.arange(channel_count, dtype=jnp.int32))
    counts = jnp.sum(
        (owner_map[None, :] == jnp.arange(owner_count, dtype=jnp.int32)[:, None]).astype(jnp.int32),
        axis=1,
    )
    starts = jnp.cumsum(counts) - counts
    slot_index = jnp.arange(slot_count, dtype=jnp.int32)
    position = jnp.clip(starts[:, None] + slot_index[None, :], 0, channel_count - 1)
    channel = jnp.take(ranking, position, axis=0)
    is_live = slot_index[None, :] < counts[:, None]
    return (channel, is_live)


def general_shards(volts, taps, owner_map, assign):
    chan_count = lax.axis_size("chan")
    rows_count = lax.axis_size("row")
    cols_count = lax.axis_size("col")
    owner_count = chan_count * cols_count
    local_inputs = volts.shape[1]
    spec_len = volts.shape[3] // NFFT - TAPS + 1
    channel, is_live = slot_table(owner_map, owner_count, CAP)
    points = jnp.arange(NFFT, dtype=jnp.int32)
    phase = (points[:, None, None] * channel.T[None, :, :] % NFFT).astype(jnp.float32) * (
        2.0 * math.pi / NFFT
    )
    weight_live = is_live.T[None, :, :].astype(jnp.float32) / math.sqrt(NFFT)
    cosine = jnp.cos(phase) * weight_live
    sine = jnp.sin(phase) * weight_live
    table = jnp.stack(
        [jnp.stack([cosine, -sine], axis=1), jnp.stack([sine, cosine], axis=1)], axis=0
    )
    total_inputs = 2 * STATIONS
    positions = jnp.arange(total_inputs, dtype=jnp.int32)
    pick = 2 * jnp.take(assign, positions // 2, axis=0) + positions % 2
    device_of = pick // local_inputs
    within = pick % local_inputs
    chan_of = device_of // (rows_count * cols_count)
    row_of = device_of // cols_count % rows_count
    col_of = device_of % cols_count
    located = ((row_of * cols_count + col_of) * chan_count + chan_of) * local_inputs + within
    row_count = total_inputs // rows_count
    row_pick = lax.dynamic_slice_in_dim(located, lax.axis_index("row") * row_count, row_count)
    total = jnp.zeros((CAP, 2 * row_count, total_inputs), jnp.float32)
    for batch in range(BATCHES):
        signal = (
            volts[batch].astype(jnp.float32).reshape(local_inputs, 2, spec_len + TAPS - 1, NFFT)
        )
        summed = jnp.zeros((local_inputs, 2, spec_len, NFFT), jnp.float32)
        for tap_index in range(TAPS):
            summed = (
                summed
                + taps[tap_index][None, None, None, :]
                * signal[:, :, tap_index : tap_index + spec_len, :]
            )
        result = jnp.einsum("iasj,ajbkg->kgibs", summed, table, precision=lax.Precision.HIGHEST)
        turned = lax.all_to_all(
            lax.all_to_all(
                result.reshape(CAP, chan_count, cols_count, local_inputs, 2 * spec_len).astype(
                    jnp.bfloat16
                ),
                "chan",
                split_axis=1,
                concat_axis=3,
                tiled=True,
            ),
            "col",
            split_axis=2,
            concat_axis=3,
            tiled=True,
        )
        gathered = lax.all_gather(turned, "row", axis=3, tiled=True)
        flat = gathered.reshape(CAP, total_inputs, -1)
        width = flat.shape[2]
        rows = jnp.take(flat, row_pick, axis=1)
        split_rows = rows.reshape(CAP, row_count, width // (2 * spec_len), 2, spec_len)
        flipped = jnp.stack(
            [split_rows[:, :, :, 1, :], -split_rows[:, :, :, 0, :]], axis=3
        ).reshape(CAP, row_count, width)
        stacked = jnp.concatenate([rows, flipped], axis=1)
        columns = jnp.take(flat, located, axis=1)
        total = total + jnp.einsum(
            "kpx,kqx->kpq", stacked, columns, preferred_element_type=jnp.float32
        )
    scale = 1.0 / math.sqrt(2 * BATCHES * spec_len)
    return (total * scale).reshape(CAP, 2, row_count, total_inputs).astype(jnp.bfloat16)


def trig_table(channels):
    points = np.arange(NFFT)
    phase = (np.arange(channels)[:, None] * points[None, :] % NFFT) * (2.0 * math.pi / NFFT)
    unit = 1.0 / math.sqrt(NFFT)
    return np.concatenate([np.cos(phase), np.sin(phase)], axis=0).astype(np.float32) * np.float32(unit)


BLOCK = 4
AHEAD = 6
LAG = 8


def spectra_kernel(batch, channels, owners, inputs, rows, spec_len,
                   owner_ref, volts_ref, taps_ref, trig_ref, out_ref,
                   wave, weight, prod, lined, count, table, sem):
    blocks = pl.cdiv(rows, BLOCK)
    parts = NFFT // LANES
    halves = 2 * channels
    pairs = spec_len // 2
    stride = lined.shape[0] // channels

    def fetch(block):
        for step in range(BLOCK):
            row = jnp.minimum(block * BLOCK + step, rows - 1)
            for part in range(parts):
                start = pl.multiple_of(row * NFFT + part * LANES, LANES)
                pltpu.make_async_copy(
                    volts_ref.at[batch, :, :, pl.ds(start, LANES)],
                    wave.at[block, part, pl.ds(step * inputs, inputs)],
                    sem.at[block],
                ).start()

    def arrived(block):
        pltpu.make_async_copy(wave.at[block], wave.at[block], sem.at[block]).wait()

    for block in range(AHEAD):
        fetch(block)

    for tap in range(TAPS):
        scaled = trig_ref[...] * taps_ref[tap:tap + 1, :]
        high = scaled.astype(jnp.bfloat16)
        low = (scaled - high.astype(jnp.float32)).astype(jnp.bfloat16)
        weight[tap * halves:(tap + 1) * halves, :NFFT] = high
        weight[tap * halves:(tap + 1) * halves, NFFT:] = low

    for owner in range(owners):
        count[owner] = 0
        for slot in range(CAP):
            table[owner * CAP + slot] = 0

    @pl.loop(0, channels)
    def _(k):
        owner = owner_ref[k]
        used = count[owner]
        table[owner * CAP + used] = k
        count[owner] = used + 1

    lane = lax.broadcasted_iota(jnp.int32, (halves, LANES), 1)
    low_half = lane < LANES // 2
    even = (lax.broadcasted_iota(jnp.int32, (channels, LANES), 1) % 2) == 0

    def tap_sum(tile, odd):
        total = prod[tile, odd * halves:(odd + 1) * halves, :]
        for e in range(1, TAPS // 2):
            m = 2 * e + odd
            total = total + prod[tile + e, m * halves:(m + 1) * halves, :]
        return total

    def finish(pair, turned):
        for step in range(2):
            tile = pair + step
            following = pltpu.roll(tap_sum(tile + 1, 1), LANES // 2, 1)
            value = tap_sum(tile, 0) + jnp.where(low_half, turned, following)
            turned = following
            cosine = value[:channels]
            sine = value[channels:]
            mixed = cosine + jnp.where(
                even, pltpu.roll(sine, LANES - 1, 1), -pltpu.roll(sine, 1, 1)
            )
            lined[pl.ds(tile, channels, stride=stride), :] = mixed
        return turned

    def body(block, turned):
        ahead = jnp.minimum(block + AHEAD, blocks - 1)

        @pl.when(block + AHEAD < blocks)
        def _():
            fetch(ahead)

        arrived(block)
        turned = finish(2 * block + LAG - 6, turned)
        x = jnp.concatenate(
            [wave.at[block, part].reshape(BLOCK * inputs * 2, LANES)[...] for part in range(parts)],
            axis=1,
        )
        y = lax.dot_general(
            weight[...], jnp.concatenate([x, x], axis=1), (((1,), (1,)), ((), ())),
            preferred_element_type=jnp.float32,
        )
        prod[2 * block + LAG] = y[:, :LANES]
        prod[2 * block + LAG + 1] = y[:, LANES:]
        return turned

    turned = lax.fori_loop(0, blocks, body, jnp.zeros((halves, LANES), jnp.float32))
    finish(2 * blocks + LAG - 6, turned)

    span = LANES // 2
    to = lax.broadcasted_iota(jnp.int32, (LANES, LANES), 0)
    source = ((to // inputs) % 2) * span + (to % inputs) * 2 + to // (2 * inputs)
    turn = (lax.broadcasted_iota(jnp.int32, (LANES, LANES), 1) == source).astype(jnp.bfloat16)
    for owner in range(owners):
        pieces = []
        for slot in range(CAP):
            k = table[owner * CAP + slot]
            pieces.append(lined[pl.ds(k * stride + LAG, pairs), :].astype(jnp.bfloat16))
        w = jnp.concatenate(pieces, axis=0)
        t = lax.dot_general(turn, w, (((1,), (1,)), ((), ())), preferred_element_type=jnp.float32)
        cols = []
        for slot in range(CAP):
            for q in range(4):
                cols.append(t[q * inputs:(q + 1) * inputs, slot * pairs:(slot + 1) * pairs])
        out_ref[owner] = jnp.concatenate(cols, axis=1).astype(jnp.bfloat16)


def spectra(batch, volts, taps, owner_map, owners):
    channels = owner_map.shape[0]
    inputs = volts.shape[1]
    rows = volts.shape[3] // NFFT
    spec_len = rows - TAPS + 1
    blocks = -(-rows // BLOCK)
    halves = 2 * channels
    parts = NFFT // LANES
    stride = 2 * blocks + LAG
    stride = -(-stride // 8) * 8
    trig = jnp.asarray(trig_table(channels))
    return pl.pallas_call(
        functools.partial(spectra_kernel, batch, channels, owners, inputs, rows, spec_len),
        out_shape=jax.ShapeDtypeStruct((owners, inputs, 2 * CAP * spec_len), jnp.bfloat16),
        in_specs=[
            pl.BlockSpec(memory_space=pltpu.SMEM),
            pl.BlockSpec(memory_space=pl.ANY),
            pl.BlockSpec(memory_space=pltpu.VMEM),
            pl.BlockSpec(memory_space=pltpu.VMEM),
        ],
        out_specs=pl.BlockSpec(memory_space=pltpu.VMEM),
        scratch_shapes=[
            pltpu.VMEM((blocks, parts, BLOCK * inputs, 2, LANES), jnp.bfloat16),
            pltpu.VMEM((TAPS * halves, 2 * NFFT), jnp.bfloat16),
            pltpu.VMEM((2 * blocks + LAG, TAPS * halves, LANES), jnp.float32),
            pltpu.VMEM((channels * stride, LANES), jnp.float32),
            pltpu.SMEM((owners,), jnp.int32),
            pltpu.SMEM((owners * CAP,), jnp.int32),
            pltpu.SemaphoreType.DMA((blocks,)),
        ],
        compiler_params=pltpu.CompilerParams(vmem_limit_bytes=48 * 1024 * 1024),
        cost_estimate=pl.CostEstimate(
            flops=4 * rows * inputs * 2 * NFFT * TAPS * halves, bytes_accessed=volts.size, transcendentals=0
        ),
        name="spectra",
    )(owner_map, volts, taps, trig)


def visibility_kernel(scale, live_ref, place_ref, mine_a, mine_b, other_a, other_b, out_ref, cols, rows):
    slot = pl.program_id(0)
    step = pl.program_id(1)
    half, width = mine_a.shape
    total = 2 * half
    group = width // CAP
    high = -(-group // LANES) * LANES
    row_count = out_ref.shape[2]

    @pl.when((slot == 0) & (step == 0))
    def _():
        for index, (mine, other) in enumerate(((mine_a, other_a), (mine_b, other_b))):
            got = jnp.dot(place_ref[:, :half], mine[...], preferred_element_type=jnp.float32)
            got = got + jnp.dot(place_ref[:, half:], other[...], preferred_element_type=jnp.float32)
            got = got.astype(jnp.bfloat16)
            cols[index] = got

    first = live_ref[1] + step * row_count
    first = pl.multiple_of(first, row_count)
    source = lax.broadcasted_iota(jnp.int32, (width, high), 0)
    target = lax.broadcasted_iota(jnp.int32, (width, high), 1)
    for s in range(CAP):
        @pl.when(slot == s)
        def _():
            base = s * (width - high)
            inside = target + base - s * group
            ok = (inside >= 0) & (inside < group)
            plain = jnp.where(ok & (source == target + base), 1.0, 0.0).astype(jnp.bfloat16)
            part = group // 2
            swapped = jnp.where(inside < part, target + base + part, target + base - part)
            sign = jnp.where(inside < part, 1.0, -1.0)
            turn = jnp.where(ok & (source == swapped), sign, 0.0).astype(jnp.bfloat16)
            re = jnp.zeros((row_count, total), jnp.float32)
            im = jnp.zeros((row_count, total), jnp.float32)
            for index in range(BATCHES):
                lead = cols[index, pl.ds(first, row_count), :]
                a = jnp.dot(lead, plain, preferred_element_type=jnp.float32).astype(jnp.bfloat16)
                f = jnp.dot(lead, turn, preferred_element_type=jnp.float32).astype(jnp.bfloat16)
                c = cols[index, :, base:base + high]
                dims = (((1,), (1,)), ((), ()))
                re = re + lax.dot_general(a, c, dims, preferred_element_type=jnp.float32)
                im = im + lax.dot_general(f, c, dims, preferred_element_type=jnp.float32)
            live = s < live_ref[0]
            out_ref[0, 0] = jnp.where(live, re * scale, 0.0).astype(jnp.bfloat16)
            out_ref[0, 1] = jnp.where(live, im * scale, 0.0).astype(jnp.bfloat16)


def visibility(scale, live, place, mine, other, row_count):
    half, width = mine[0].shape
    total = 2 * half
    block = 128
    return pl.pallas_call(
        functools.partial(visibility_kernel, scale),
        out_shape=jax.ShapeDtypeStruct((CAP, 2, row_count, total), jnp.bfloat16),
        grid=(CAP, row_count // block),
        in_specs=[pl.BlockSpec(memory_space=pltpu.SMEM)]
        + [pl.BlockSpec(memory_space=pltpu.VMEM)] * 5,
        out_specs=pl.BlockSpec((1, 2, block, total), lambda s, p: (s, 0, p, 0)),
        scratch_shapes=[
            pltpu.VMEM((BATCHES, total, width), jnp.bfloat16),
            pltpu.VMEM((8, LANES), jnp.float32),
        ],
        compiler_params=pltpu.CompilerParams(vmem_limit_bytes=48 * 1024 * 1024),
        name="visibility",
    )(live, place, *mine, *other)


def tiled_shards(volts, taps, owner_map, assign):
    chan_count = lax.axis_size("chan")
    rows_count = lax.axis_size("row")
    cols_count = lax.axis_size("col")
    owners = chan_count * cols_count
    inputs = volts.shape[1]
    spec_len = volts.shape[3] // NFFT - TAPS + 1
    my_row = lax.axis_index("row")
    me = lax.axis_index("chan") * cols_count + lax.axis_index("col")
    total_inputs = 2 * STATIONS
    row_count = total_inputs // rows_count
    positions = jnp.arange(total_inputs, dtype=jnp.int32)
    pick = 2 * jnp.repeat(assign, 2) + positions % 2
    device_of = pick // inputs
    within = pick % inputs
    chan_of = device_of // (rows_count * cols_count)
    row_of = device_of // cols_count % rows_count
    col_of = device_of % cols_count
    located = (
        jnp.where(row_of == my_row, 0, owners) + chan_of * cols_count + col_of
    ) * inputs + within
    place = (located[:, None] == positions[None, :]).astype(jnp.bfloat16)
    owned = jnp.sum((owner_map == me).astype(jnp.int32))
    live = jnp.stack([owned, my_row * row_count])
    mine = []
    other = []
    for batch in range(BATCHES):
        sent = spectra(batch, volts, taps, owner_map, owners)
        turned = lax.all_to_all(sent, ("chan", "col"), split_axis=0, concat_axis=0, tiled=True)
        flat = turned.reshape(owners * inputs, -1)
        mine.append(flat)
        other.append(lax.ppermute(flat, "row", [(0, 1), (1, 0)]))
    scale = 1.0 / math.sqrt(2 * BATCHES * spec_len)
    return visibility(scale, live, place, mine, other, row_count)


def solution(mesh):
    placed = (P(None, ("chan", "row", "col"), None, None), P(), P(), P())

    def shards(volts, taps, owner_map, assign):
        if 4 * volts.shape[1] == LANES and mesh.shape["row"] == 2:
            return tiled_shards(volts, taps, owner_map, assign)
        return general_shards(volts, taps, owner_map, assign)

    return jax.shard_map(
        shards,
        mesh=mesh,
        in_specs=placed,
        out_specs=P(("chan", "col"), None, "row", None),
        check_vma=False,
    )
```

```python
import functools
import math

import jax
import jax.numpy as jnp
import numpy as np
from jax import lax
from jax.experimental import pallas as pl
from jax.experimental.pallas import tpu as pltpu
from jax.sharding import PartitionSpec as P

STATIONS = 512
NFFT = 512
TAPS = 8
BATCHES = 2
CAP = 2
LANES = 128


def slot_table(owner_map, owner_count, slot_count):
    channel_count = owner_map.shape[0]
    ranking = jnp.argsort(owner_map * channel_count + jnp.arange(channel_count, dtype=jnp.int32))
    counts = jnp.sum(
        (owner_map[None, :] == jnp.arange(owner_count, dtype=jnp.int32)[:, None]).astype(jnp.int32),
        axis=1,
    )
    starts = jnp.cumsum(counts) - counts
    slot_index = jnp.arange(slot_count, dtype=jnp.int32)
    position = jnp.clip(starts[:, None] + slot_index[None, :], 0, channel_count - 1)
    channel = jnp.take(ranking, position, axis=0)
    is_live = slot_index[None, :] < counts[:, None]
    return (channel, is_live)


def general_shards(volts, taps, owner_map, assign):
    chan_count = lax.axis_size("chan")
    rows_count = lax.axis_size("row")
    cols_count = lax.axis_size("col")
    owner_count = chan_count * cols_count
    local_inputs = volts.shape[1]
    spec_len = volts.shape[3] // NFFT - TAPS + 1
    channel, is_live = slot_table(owner_map, owner_count, CAP)
    points = jnp.arange(NFFT, dtype=jnp.int32)
    phase = (points[:, None, None] * channel.T[None, :, :] % NFFT).astype(jnp.float32) * (
        2.0 * math.pi / NFFT
    )
    weight_live = is_live.T[None, :, :].astype(jnp.float32) / math.sqrt(NFFT)
    cosine = jnp.cos(phase) * weight_live
    sine = jnp.sin(phase) * weight_live
    table = jnp.stack(
        [jnp.stack([cosine, -sine], axis=1), jnp.stack([sine, cosine], axis=1)], axis=0
    )
    total_inputs = 2 * STATIONS
    positions = jnp.arange(total_inputs, dtype=jnp.int32)
    pick = 2 * jnp.take(assign, positions // 2, axis=0) + positions % 2
    device_of = pick // local_inputs
    within = pick % local_inputs
    chan_of = device_of // (rows_count * cols_count)
    row_of = device_of // cols_count % rows_count
    col_of = device_of % cols_count
    located = ((row_of * cols_count + col_of) * chan_count + chan_of) * local_inputs + within
    row_count = total_inputs // rows_count
    row_pick = lax.dynamic_slice_in_dim(located, lax.axis_index("row") * row_count, row_count)
    total = jnp.zeros((CAP, 2 * row_count, total_inputs), jnp.float32)
    for batch in range(BATCHES):
        signal = (
            volts[batch].astype(jnp.float32).reshape(local_inputs, 2, spec_len + TAPS - 1, NFFT)
        )
        summed = jnp.zeros((local_inputs, 2, spec_len, NFFT), jnp.float32)
        for tap_index in range(TAPS):
            summed = (
                summed
                + taps[tap_index][None, None, None, :]
                * signal[:, :, tap_index : tap_index + spec_len, :]
            )
        result = jnp.einsum("iasj,ajbkg->kgibs", summed, table, precision=lax.Precision.HIGHEST)
        turned = lax.all_to_all(
            lax.all_to_all(
                result.reshape(CAP, chan_count, cols_count, local_inputs, 2 * spec_len).astype(
                    jnp.bfloat16
                ),
                "chan",
                split_axis=1,
                concat_axis=3,
                tiled=True,
            ),
            "col",
            split_axis=2,
            concat_axis=3,
            tiled=True,
        )
        gathered = lax.all_gather(turned, "row", axis=3, tiled=True)
        flat = gathered.reshape(CAP, total_inputs, -1)
        width = flat.shape[2]
        rows = jnp.take(flat, row_pick, axis=1)
        split_rows = rows.reshape(CAP, row_count, width // (2 * spec_len), 2, spec_len)
        flipped = jnp.stack(
            [split_rows[:, :, :, 1, :], -split_rows[:, :, :, 0, :]], axis=3
        ).reshape(CAP, row_count, width)
        stacked = jnp.concatenate([rows, flipped], axis=1)
        columns = jnp.take(flat, located, axis=1)
        total = total + jnp.einsum(
            "kpx,kqx->kpq", stacked, columns, preferred_element_type=jnp.float32
        )
    scale = 1.0 / math.sqrt(2 * BATCHES * spec_len)
    return (total * scale).reshape(CAP, 2, row_count, total_inputs).astype(jnp.bfloat16)


def trig_table(channels):
    points = np.arange(NFFT)
    phase = (np.arange(channels)[:, None] * points[None, :] % NFFT) * (2.0 * math.pi / NFFT)
    unit = 1.0 / math.sqrt(NFFT)
    return np.concatenate([np.cos(phase), np.sin(phase)], axis=0).astype(np.float32) * np.float32(unit)


BLOCK = 4
MXU = 256
UNROLL = 2
UNIT = 16
ORDER = ((0, 1, 2, 0, 1, 2, 0, 1), (0, 1, 0, 2, 2, 1, 0, 1))
LAYOUT = (
    ((0, 0, (0, 1, 2)), (0, 1, (3, 4, 5)), (0, 2, (6, 7))),
    ((1, 3, (4, 6, 7)), (0, 3, (0, 1, 2)), (0, 2, (5,)), (1, 2, (3,))),
    ((1, 0, (0, 1, 3)), (1, 1, (2, 4, 5)), (1, 2, (6, 7))),
)
LAG = 8


def spectra_kernel(batch, channels, owners, inputs, rows, spec_len,
                   owner_hbm, volts_ref, taps_hbm, trig_hbm, out_ref,
                   wave, weight, prod, lined, taps_ref, trig_ref,
                   owner_ref, count, table, sem, small):
    blocks = wave.shape[0]
    halves = 2 * channels
    pairs = spec_len // 2
    stride = lined.shape[0] // channels
    lanes = 2 * inputs
    source = volts_ref.at[batch].reshape(lanes, volts_ref.shape[3])

    loads = [
        pltpu.make_async_copy(taps_hbm, taps_ref, small.at[0]),
        pltpu.make_async_copy(trig_hbm, trig_ref, small.at[1]),
        pltpu.make_async_copy(owner_hbm, owner_ref, small.at[2]),
    ]
    for load in loads:
        load.start()

    @pl.loop(0, blocks)
    def _(block):
        for step in range(BLOCK):
            row = jnp.minimum(block * BLOCK + step, rows - 1)
            start = pl.multiple_of(row * NFFT, NFFT)
            pltpu.make_async_copy(
                source.at[:, pl.ds(start, NFFT)],
                wave.at[block, pl.ds(step * lanes, lanes)],
                sem.at[block],
            ).start()

    for load in loads:
        load.wait()

    for tap in range(TAPS):
        scaled = trig_ref[...] * taps_ref[tap:tap + 1, :]
        high = scaled.astype(jnp.bfloat16)
        low = (scaled - high.astype(jnp.float32)).astype(jnp.bfloat16)
        weight[tap * halves:(tap + 1) * halves, :NFFT] = high
        weight[tap * halves:(tap + 1) * halves, NFFT:] = low

    for owner in range(owners):
        count[owner] = 0
        for slot in range(CAP):
            table[owner * CAP + slot] = 0
    table[owners * CAP] = 0

    lane = lax.broadcasted_iota(jnp.int32, (halves, LANES), 1)
    low_half = lane < LANES // 2
    even = (lax.broadcasted_iota(jnp.int32, (channels, LANES), 1) % 2) == 0

    def tap_sum(tile, odd):
        total = prod[tile, odd * halves:(odd + 1) * halves, :]
        for e in range(1, TAPS // 2):
            m = 2 * e + odd
            total = total + prod[tile + e, m * halves:(m + 1) * halves, :]
        return total

    def finish(pair, turned):
        for step in range(2 * UNROLL):
            tile = pair + step
            following = pltpu.roll(tap_sum(tile + 1, 1), LANES // 2, 1)
            value = tap_sum(tile, 0) + jnp.where(low_half, turned, following)
            turned = following
            cosine = value[:channels]
            sine = value[channels:]
            mixed = cosine + jnp.where(
                even, pltpu.roll(sine, LANES - 1, 1), -pltpu.roll(sine, 1, 1)
            )
            lined[pl.ds(tile, channels, stride=stride), :] = mixed
        return turned

    def place(k):
        real = k < channels
        owner = owner_ref[jnp.minimum(k, channels - 1)]
        used = count[owner]
        table[jnp.where(real, owner * CAP + used, owners * CAP)] = k
        count[owner] = jnp.where(real, used + 1, used)

    def wait(first):
        for step in range(UNROLL):
            pltpu.make_async_copy(wave.at[first + step], wave.at[first + step], sem.at[first + step]).wait()

    def stage(first, part):
        for step in range(UNROLL):
            x = wave[first + step, :, part * MXU:(part + 1) * MXU]
            pltpu.matmul_push_rhs(x, part, step, transpose=True)

    def multiply(totals, following):
        for part in range(NFFT // MXU):
            for total in totals:
                pltpu.matmul_acc_lhs(
                    total, weight[:, part * MXU:(part + 1) * MXU], load_staged_rhs=part
                )
            if following is not None:
                stage(following, part)
            for total in totals:
                pltpu.matmul_acc_lhs(
                    total, weight[:, NFFT + part * MXU:NFFT + (part + 1) * MXU]
                )

    def collect(first, totals):
        for step, total in enumerate(totals):
            y = pltpu.matmul_pop(total)
            prod[2 * (first + step) + LAG] = y[:, :LANES]
            prod[2 * (first + step) + LAG + 1] = y[:, LANES:]

    def run(*totals):
        even_totals = totals[:2]
        odd_totals = totals[2:]

        rounds = blocks // (2 * UNROLL) - 1
        share = pl.cdiv(channels, rounds)

        def body(group, turned):
            first = group * 2 * UNROLL
            wait(first + 2 * UNROLL)
            wait(first + 3 * UNROLL)
            for extra in range(share):
                place(group * share + extra)
            multiply(odd_totals, first + 2 * UNROLL)
            turned = finish(2 * first + LAG - 4 - 2 * UNROLL, turned)
            collect(first, even_totals)
            multiply(even_totals, first + 3 * UNROLL)
            turned = finish(2 * first + LAG - 4, turned)
            collect(first + UNROLL, odd_totals)
            return turned

        wait(0)
        wait(UNROLL)
        for part in range(NFFT // MXU):
            stage(0, part)
        multiply(even_totals, UNROLL)
        turned = lax.fori_loop(0, rounds, body, jnp.zeros((halves, LANES), jnp.float32))
        first = rounds * 2 * UNROLL
        wait(first + 2 * UNROLL)
        multiply(odd_totals, first + 2 * UNROLL)
        turned = finish(2 * first + LAG - 4 - 2 * UNROLL, turned)
        collect(first, even_totals)
        multiply(even_totals, None)
        turned = finish(2 * first + LAG - 4, turned)
        collect(first + UNROLL, odd_totals)
        turned = finish(2 * first + LAG - 4 + 2 * UNROLL, turned)
        collect(first + 2 * UNROLL, even_totals)
        finish(2 * first + LAG - 4 + 4 * UNROLL, turned)

    shape = (TAPS * halves, MXU)
    pl.run_scoped(run, *(pltpu.ACC(mxu_id=index % 2)(shape, jnp.float32) for index in range(4)))

    to = lax.broadcasted_iota(jnp.int32, (2 * LANES, MXU), 0)
    at = lax.broadcasted_iota(jnp.int32, (2 * LANES, MXU), 1)
    row = to % LANES
    origin = ((row // inputs) % 2) * lanes + (row % inputs) * 2 + row // lanes + to - row
    turn = (at == origin).astype(jnp.bfloat16)
    unit = lax.broadcasted_iota(jnp.int32, (inputs, LANES), 1) // UNIT

    def pick(choices, tile):
        value = None
        for column, group, units in choices:
            piece = tile[group * inputs:(group + 1) * inputs, column * LANES:(column + 1) * LANES]
            if value is None:
                value = piece
            else:
                inside = functools.reduce(jnp.logical_or, [unit == u for u in units])
                value = jnp.where(inside, piece, value)
        return value

    def deal(*totals):
        for pair in range(owners // 2):
            total = totals[pair % len(totals)]
            sides = []
            for side in range(2):
                owner = 2 * pair + side
                pieces = []
                for slot in range(CAP):
                    first = table[owner * CAP + slot] * stride + LAG
                    for u in ORDER[slot]:
                        start = pl.multiple_of(first + u * UNIT, 8)
                        pieces.append(lined[pl.ds(start, UNIT), :].astype(jnp.bfloat16))
                sides.append(jnp.concatenate(pieces, axis=0))
            pltpu.matmul_push_rhs(
                jnp.concatenate(sides, axis=1), pair // 2 % 2, pair % 2, transpose=True
            )
            pltpu.matmul_acc_lhs(total, turn, load_staged_rhs=pair // 2 % 2)
            dealt = pltpu.matmul_pop(total)
            for side in range(2):
                tile = dealt[side * LANES:(side + 1) * LANES]
                out_ref[2 * pair + side] = jnp.concatenate(
                    [pick(choices, tile).astype(jnp.bfloat16) for choices in LAYOUT], axis=1
                )

    pl.run_scoped(
        deal, *(pltpu.ACC(mxu_id=index % 2)((2 * LANES, MXU), jnp.float32) for index in range(4))
    )


def spectra(batch, volts, taps, owner_map, owners):
    channels = owner_map.shape[0]
    inputs = volts.shape[1]
    rows = volts.shape[3] // NFFT
    spec_len = rows - TAPS + 1
    blocks = -(-rows // BLOCK)
    halves = 2 * channels
    stride = 2 * blocks + LAG
    stride = -(-stride // 8) * 8
    trig = jnp.asarray(trig_table(channels))
    hbm = pl.BlockSpec(memory_space=pltpu.HBM)
    return pl.pallas_call(
        functools.partial(spectra_kernel, batch, channels, owners, inputs, rows, spec_len),
        out_shape=jax.ShapeDtypeStruct((owners, inputs, 2 * CAP * spec_len), jnp.bfloat16),
        in_specs=[hbm] * 4,
        out_specs=pl.BlockSpec(memory_space=pltpu.VMEM),
        scratch_shapes=[
            pltpu.VMEM((blocks, BLOCK * inputs * 2, NFFT), jnp.bfloat16),
            pltpu.VMEM((TAPS * halves, 2 * NFFT), jnp.bfloat16),
            pltpu.VMEM((2 * blocks + LAG, TAPS * halves, LANES), jnp.float32),
            pltpu.VMEM((channels * stride, LANES), jnp.float32),
            pltpu.VMEM(taps.shape, jnp.float32),
            pltpu.VMEM(trig.shape, jnp.float32),
            pltpu.SMEM((channels,), jnp.int32),
            pltpu.SMEM((owners,), jnp.int32),
            pltpu.SMEM((owners * CAP + 1,), jnp.int32),
            pltpu.SemaphoreType.DMA((blocks,)),
            pltpu.SemaphoreType.DMA((3,)),
        ],
        compiler_params=pltpu.CompilerParams(vmem_limit_bytes=48 * 1024 * 1024),
        cost_estimate=pl.CostEstimate(
            flops=4 * rows * inputs * 2 * NFFT * TAPS * halves, bytes_accessed=volts.size, transcendentals=0
        ),
        name="spectra",
    )(*(pltpu.with_memory_space_constraint(x, pltpu.HBM) for x in (owner_map, volts, taps, trig)))


def lane_tables():
    window = 2 * LANES
    held = {}
    for tile, choices in enumerate(LAYOUT):
        for slot, quarter, units in choices:
            for u in units:
                for offset in range(UNIT):
                    lane = tile * LANES + u * UNIT + offset
                    held[slot, quarter, ORDER[slot][u], offset] = lane
    keep = np.zeros((CAP, UNIT, window), np.float32)
    turn = np.zeros((CAP, window, window), np.float32)
    for (slot, quarter, third, offset), lane in held.items():
        base = slot * LANES
        other = held[slot, (quarter + 2) % 4, third, offset]
        keep[slot, :, lane - base] = 1.0
        turn[slot, other - base, lane - base] = 1.0 if quarter < 2 else -1.0
    return keep, turn


def visibility_kernel(scale, owner_ref, place_ref, keep_ref, turn_ref,
                      mine_a, mine_b, other_a, other_b, out_ref, cols, lead):
    slot = pl.program_id(0)
    step = pl.program_id(1)
    half = mine_a.shape[0]
    row_count = out_ref.shape[2]
    block = out_ref.shape[3]
    window = turn_ref.shape[1]
    dims = (((1,), (1,)), ((), ()))

    @pl.when((slot == 0) & (step == 0))
    def _():
        for index, (mine, other) in enumerate(((mine_a, other_a), (mine_b, other_b))):
            got = jnp.dot(place_ref[:, :half], mine[...], preferred_element_type=jnp.float32)
            got = got + jnp.dot(place_ref[:, half:], other[...], preferred_element_type=jnp.float32)
            cols[index] = got.astype(jnp.bfloat16)
        first = pl.multiple_of(lax.axis_index("row") * row_count, row_count)
        for s in range(CAP):
            for index in range(BATCHES):
                rows = cols[index, pl.ds(first, row_count), s * LANES:s * LANES + window]
                lead[s, index, :row_count] = rows * keep_ref[s, :1]
                lead[s, index, row_count:] = jnp.dot(
                    rows, turn_ref[s], preferred_element_type=jnp.float32
                ).astype(jnp.bfloat16)

    me = lax.axis_index("chan") * lax.axis_size("col") + lax.axis_index("col")
    owned = jnp.int32(0)
    for k in range(owner_ref.shape[0]):
        owned = owned + jnp.where(owner_ref[k] == me, 1, 0)
    factor = jnp.where(slot < owned, jnp.float32(scale), jnp.float32(0.0))
    at = pl.multiple_of(step * block, block)
    for s in range(CAP):
        @pl.when(slot == s)
        def _():
            value = None
            for index in range(BATCHES):
                c = cols[index, pl.ds(at, block), s * LANES:s * LANES + window]
                term = lax.dot_general(lead[s, index], c, dims, preferred_element_type=jnp.float32)
                value = term if value is None else value + term
            value = (value * factor).astype(jnp.bfloat16)
            out_ref[0, 0] = value[:row_count]
            out_ref[0, 1] = value[row_count:]


def visibility(scale, owner_map, place, mine, other, row_count):
    half, width = mine[0].shape
    total = 2 * half
    block = 256
    keep, turn = (jnp.asarray(t, jnp.bfloat16) for t in lane_tables())
    return pl.pallas_call(
        functools.partial(visibility_kernel, scale),
        out_shape=jax.ShapeDtypeStruct((CAP, 2, row_count, total), jnp.bfloat16),
        grid=(CAP, total // block),
        in_specs=[pl.BlockSpec(memory_space=pltpu.SMEM)]
        + [pl.BlockSpec(memory_space=pltpu.VMEM)] * 7,
        out_specs=pl.BlockSpec((1, 2, row_count, block), lambda s, p: (s, 0, 0, p)),
        scratch_shapes=[
            pltpu.VMEM((BATCHES, total, width), jnp.bfloat16),
            pltpu.VMEM((CAP, BATCHES, 2 * row_count, 2 * LANES), jnp.bfloat16),
        ],
        compiler_params=pltpu.CompilerParams(vmem_limit_bytes=48 * 1024 * 1024),
        name="visibility",
    )(owner_map, place, keep, turn, *mine, *other)


def tiled_shards(volts, taps, owner_map, assign):
    chan_count = lax.axis_size("chan")
    rows_count = lax.axis_size("row")
    cols_count = lax.axis_size("col")
    owners = chan_count * cols_count
    inputs = volts.shape[1]
    spec_len = volts.shape[3] // NFFT - TAPS + 1
    my_row = lax.axis_index("row")
    total_inputs = 2 * STATIONS
    row_count = total_inputs // rows_count
    positions = jnp.arange(total_inputs, dtype=jnp.int32)
    pick = 2 * jnp.repeat(assign, 2) + positions % 2
    device_of = pick // inputs
    within = pick % inputs
    chan_of = device_of // (rows_count * cols_count)
    row_of = device_of // cols_count % rows_count
    col_of = device_of % cols_count
    located = (
        jnp.where(row_of == my_row, 0, owners) + chan_of * cols_count + col_of
    ) * inputs + within
    place = (located[:, None] == positions[None, :]).astype(jnp.bfloat16)
    mine = []
    other = []
    for batch in range(BATCHES):
        sent = spectra(batch, volts, taps, owner_map, owners)
        turned = lax.all_to_all(sent, ("chan", "col"), split_axis=0, concat_axis=0, tiled=True)
        flat = turned.reshape(owners * inputs, -1)
        mine.append(flat)
        other.append(lax.ppermute(flat, "row", [(0, 1), (1, 0)]))
    scale = 1.0 / math.sqrt(2 * BATCHES * spec_len)
    return visibility(scale, owner_map, place, mine, other, row_count)


def fits(volts, owner_map, mesh):
    rows = volts.shape[3] // NFFT
    return (
        4 * volts.shape[1] == LANES
        and mesh.shape["row"] == 2
        and rows - TAPS + 1 == 6 * UNIT
        and -(-rows // BLOCK) % (2 * UNROLL) == UNROLL
        and owner_map.shape[0] % 8 == 0
        and TAPS * 2 * owner_map.shape[0] <= 384
    )


def solution(mesh):
    placed = (P(None, ("chan", "row", "col"), None, None), P(), P(), P())

    def shards(volts, taps, owner_map, assign):
        if fits(volts, owner_map, mesh):
            return tiled_shards(volts, taps, owner_map, assign)
        return general_shards(volts, taps, owner_map, assign)

    return jax.shard_map(
        shards,
        mesh=mesh,
        in_specs=placed,
        out_specs=P(("chan", "col"), None, "row", None),
        check_vma=False,
    )
```

```python
import functools
import math

import jax
import jax.numpy as jnp
import numpy as np
from jax import lax
from jax.experimental import pallas as pl
from jax.experimental.pallas import tpu as pltpu
from jax.sharding import PartitionSpec as P


STATIONS = 512
NFFT = 512
TAPS = 8
BATCHES = 2
CAP = 2
LANES = 128


def slot_table(owner_map, owner_count, slot_count):
    channel_count = owner_map.shape[0]
    ranking = jnp.argsort(owner_map * channel_count + jnp.arange(channel_count, dtype=jnp.int32))
    counts = jnp.sum(
        (owner_map[None, :] == jnp.arange(owner_count, dtype=jnp.int32)[:, None]).astype(jnp.int32),
        axis=1,
    )
    starts = jnp.cumsum(counts) - counts
    slot_index = jnp.arange(slot_count, dtype=jnp.int32)
    position = jnp.clip(starts[:, None] + slot_index[None, :], 0, channel_count - 1)
    channel = jnp.take(ranking, position, axis=0)
    is_live = slot_index[None, :] < counts[:, None]
    return (channel, is_live)


def general_shards(volts, taps, owner_map, assign):
    chan_count = lax.axis_size("chan")
    rows_count = lax.axis_size("row")
    cols_count = lax.axis_size("col")
    owner_count = chan_count * cols_count
    local_inputs = volts.shape[1]
    spec_len = volts.shape[3] // NFFT - TAPS + 1
    channel, is_live = slot_table(owner_map, owner_count, CAP)
    points = jnp.arange(NFFT, dtype=jnp.int32)
    phase = (points[:, None, None] * channel.T[None, :, :] % NFFT).astype(jnp.float32) * (
        2.0 * math.pi / NFFT
    )
    weight_live = is_live.T[None, :, :].astype(jnp.float32) / math.sqrt(NFFT)
    cosine = jnp.cos(phase) * weight_live
    sine = jnp.sin(phase) * weight_live
    table = jnp.stack(
        [jnp.stack([cosine, -sine], axis=1), jnp.stack([sine, cosine], axis=1)], axis=0
    )
    total_inputs = 2 * STATIONS
    positions = jnp.arange(total_inputs, dtype=jnp.int32)
    pick = 2 * jnp.take(assign, positions // 2, axis=0) + positions % 2
    device_of = pick // local_inputs
    within = pick % local_inputs
    chan_of = device_of // (rows_count * cols_count)
    row_of = device_of // cols_count % rows_count
    col_of = device_of % cols_count
    located = ((row_of * cols_count + col_of) * chan_count + chan_of) * local_inputs + within
    row_count = total_inputs // rows_count
    row_pick = lax.dynamic_slice_in_dim(located, lax.axis_index("row") * row_count, row_count)
    total = jnp.zeros((CAP, 2 * row_count, total_inputs), jnp.float32)
    for batch in range(BATCHES):
        signal = (
            volts[batch].astype(jnp.float32).reshape(local_inputs, 2, spec_len + TAPS - 1, NFFT)
        )
        summed = jnp.zeros((local_inputs, 2, spec_len, NFFT), jnp.float32)
        for tap_index in range(TAPS):
            summed = (
                summed
                + taps[tap_index][None, None, None, :]
                * signal[:, :, tap_index : tap_index + spec_len, :]
            )
        result = jnp.einsum("iasj,ajbkg->kgibs", summed, table, precision=lax.Precision.HIGHEST)
        turned = lax.all_to_all(
            lax.all_to_all(
                result.reshape(CAP, chan_count, cols_count, local_inputs, 2 * spec_len).astype(
                    jnp.bfloat16
                ),
                "chan",
                split_axis=1,
                concat_axis=3,
                tiled=True,
            ),
            "col",
            split_axis=2,
            concat_axis=3,
            tiled=True,
        )
        gathered = lax.all_gather(turned, "row", axis=3, tiled=True)
        flat = gathered.reshape(CAP, total_inputs, -1)
        width = flat.shape[2]
        rows = jnp.take(flat, row_pick, axis=1)
        split_rows = rows.reshape(CAP, row_count, width // (2 * spec_len), 2, spec_len)
        flipped = jnp.stack(
            [split_rows[:, :, :, 1, :], -split_rows[:, :, :, 0, :]], axis=3
        ).reshape(CAP, row_count, width)
        stacked = jnp.concatenate([rows, flipped], axis=1)
        columns = jnp.take(flat, located, axis=1)
        total = total + jnp.einsum(
            "kpx,kqx->kpq", stacked, columns, preferred_element_type=jnp.float32
        )
    scale = 1.0 / math.sqrt(2 * BATCHES * spec_len)
    return (total * scale).reshape(CAP, 2, row_count, total_inputs).astype(jnp.bfloat16)


def trig_table(channels):
    points = np.arange(NFFT)
    phase = (np.arange(channels)[:, None] * points[None, :] % NFFT) * (2.0 * math.pi / NFFT)
    unit = 1.0 / math.sqrt(NFFT)
    return np.concatenate([np.cos(phase), np.sin(phase)], axis=0).astype(np.float32) * np.float32(unit)


BLOCK = 4
MXU = 256
UNROLL = 2
UNIT = 16
ORDER = (0, 1, 2, 2, 0, 1, 2, 2)
WHOLE = ((0, (0, 1, 2)), (1, (3,)), (2, (4, 5, 6)), (3, (7,)))
HALF = ((1, (0, 1)), (3, (4, 5)))
LAG = 8


def spectra_kernel(segments, channels, owners, columns, inputs, rows,
                   owner_hbm, volts_ref, taps_hbm, trig_hbm, out_ref,
                   wave, weight, prod, lined, taps_ref, trig_ref,
                   owner_ref, count, table, sem, small):
    blocks = wave.shape[0]
    sets = blocks // UNROLL
    rounds = (sets - 3) // 2
    halves = 2 * channels
    stride = lined.shape[0] // channels
    lanes = 2 * inputs

    loads = [
        pltpu.make_async_copy(taps_hbm, taps_ref, small.at[0]),
        pltpu.make_async_copy(trig_hbm, trig_ref, small.at[1]),
        pltpu.make_async_copy(owner_hbm, owner_ref, small.at[2]),
    ]
    for load in loads:
        load.start()

    units = []
    fetches = []
    for batch, first_row, spectra_count in segments:
        source = volts_ref.at[batch].reshape(lanes, volts_ref.shape[3])
        for u in range(spectra_count // (2 * UNIT)):
            units.append(2 * len(fetches) + u * UNIT)
        for block in range(-(-(spectra_count + TAPS - 1) // BLOCK)):
            fetches.append((source, first_row + block * BLOCK))

    def fetch(block):
        source, row = fetches[block]
        whole = min(BLOCK, rows - row)
        pieces = [(0, row, whole)] + [(step, rows - 1, 1) for step in range(whole, BLOCK)]
        for step, start, held in pieces:
            pltpu.make_async_copy(
                source.at[:, start * NFFT:(start + held) * NFFT],
                wave.at[block, :, step * NFFT:(step + held) * NFFT],
                sem.at[block],
            ).start()

    for block in range(blocks):
        fetch(block)

    for load in loads:
        load.wait()

    for tap in range(TAPS):
        scaled = trig_ref[...] * taps_ref[tap:tap + 1, :]
        high = scaled.astype(jnp.bfloat16)
        low = (scaled - high.astype(jnp.float32)).astype(jnp.bfloat16)
        weight[tap * halves:(tap + 1) * halves, :NFFT] = high
        weight[tap * halves:(tap + 1) * halves, NFFT:] = low

    for owner in range(owners):
        count[owner] = 0
        for slot in range(CAP):
            table[owner * CAP + slot] = 0
    table[owners * CAP] = 0

    lane = lax.broadcasted_iota(jnp.int32, (halves, LANES), 1)
    low_half = lane < LANES // 2
    even = (lax.broadcasted_iota(jnp.int32, (channels, LANES), 1) % 2) == 0

    def tap_sum(tile, odd):
        total = prod[tile, odd * halves:(odd + 1) * halves, :]
        for e in range(1, TAPS // 2):
            m = 2 * e + odd
            total = total + prod[tile + e, m * halves:(m + 1) * halves, :]
        return total

    def finish(pair, turned):
        for step in range(2 * UNROLL):
            tile = pair + step
            following = pltpu.roll(tap_sum(tile + 1, 1), LANES // 2, 1)
            value = tap_sum(tile, 0) + jnp.where(low_half, turned, following)
            turned = following
            cosine = value[:channels]
            sine = value[channels:]
            mixed = cosine + jnp.where(
                even, pltpu.roll(sine, LANES - 1, 1), -pltpu.roll(sine, 1, 1)
            )
            lined[pl.ds(tile, channels, stride=stride), :] = mixed
        return turned

    def place(k):
        real = k < channels
        owner = owner_ref[jnp.minimum(k, channels - 1)]
        used = count[owner]
        table[jnp.where(real, owner * CAP + used, owners * CAP)] = k
        count[owner] = jnp.where(real, used + 1, used)

    def wait(first):
        for step in range(UNROLL):
            pltpu.make_async_copy(wave.at[first + step], wave.at[first + step], sem.at[first + step]).wait()

    def stage(first, part):
        for step in range(UNROLL):
            x = [
                wave[first + step, :, row * NFFT + part * MXU:row * NFFT + (part + 1) * MXU]
                for row in range(BLOCK)
            ]
            pltpu.matmul_push_rhs(jnp.concatenate(x, axis=0), part, step, transpose=True)

    def multiply(totals, following):
        for part in range(NFFT // MXU):
            for total in totals:
                pltpu.matmul_acc_lhs(
                    total, weight[:, part * MXU:(part + 1) * MXU], load_staged_rhs=part
                )
            if following is not None:
                stage(following, part)
            for total in totals:
                pltpu.matmul_acc_lhs(
                    total, weight[:, NFFT + part * MXU:NFFT + (part + 1) * MXU]
                )

    def collect(first, totals):
        for step, total in enumerate(totals):
            y = pltpu.matmul_pop(total)
            prod[2 * (first + step) + LAG] = y[:, :LANES]
            prod[2 * (first + step) + LAG + 1] = y[:, LANES:]

    def run(*totals):
        even_totals = totals[:2]
        odd_totals = totals[2:]

        share = pl.cdiv(channels, rounds)

        def body(group, turned):
            first = group * 2 * UNROLL
            wait(first + 2 * UNROLL)
            wait(first + 3 * UNROLL)
            for extra in range(share):
                place(group * share + extra)
            multiply(odd_totals, first + 2 * UNROLL)
            turned = finish(2 * first + LAG - 4 - 2 * UNROLL, turned)
            collect(first, even_totals)
            multiply(even_totals, first + 3 * UNROLL)
            turned = finish(2 * first + LAG - 4, turned)
            collect(first + UNROLL, odd_totals)
            return turned

        wait(0)
        wait(UNROLL)
        for part in range(NFFT // MXU):
            stage(0, part)
        multiply(even_totals, UNROLL)
        turned = lax.fori_loop(0, rounds, body, jnp.zeros((halves, LANES), jnp.float32))
        for index in range(2 * rounds + 1, sets):
            if index + 1 < sets:
                wait((index + 1) * UNROLL)
            multiply(
                (even_totals, odd_totals)[index % 2],
                (index + 1) * UNROLL if index + 1 < sets else None,
            )
            turned = finish(4 * (index - 1) + LAG - 8, turned)
            collect((index - 1) * UNROLL, (even_totals, odd_totals)[1 - index % 2])
        turned = finish(4 * (sets - 1) + LAG - 8, turned)
        collect((sets - 1) * UNROLL, (even_totals, odd_totals)[(sets - 1) % 2])
        finish(4 * sets + LAG - 8, turned)

    shape = (TAPS * halves, MXU)
    pl.run_scoped(run, *(pltpu.ACC(mxu_id=index % 2)(shape, jnp.float32) for index in range(4)))

    stations = inputs // 2
    to = lax.broadcasted_iota(jnp.int32, (2 * LANES, MXU), 0)
    at = lax.broadcasted_iota(jnp.int32, (2 * LANES, MXU), 1)
    row = to % LANES
    quarter = row // stations % 4
    origin = (
        quarter % 2 * lanes + (row % stations * 2 + row // (4 * stations)) * 2 + quarter // 2
        + to - row
    )
    turn = (at == origin).astype(jnp.bfloat16)
    spot = lax.broadcasted_iota(jnp.int32, (stations, LANES), 1) // UNIT
    shared = spot % 4 < 2

    def pick(choices, dealt):
        value = None
        for quarter, spots in choices:
            piece = dealt[quarter * stations:(quarter + 1) * stations]
            if value is None:
                value = piece
            else:
                inside = functools.reduce(jnp.logical_or, [spot == u for u in spots])
                value = jnp.where(inside, piece, value)
        return value

    def deal(*totals):
        for pair in range(owners // 2):
            total = totals[pair % len(totals)]
            sides = []
            for side in range(2):
                owner = 2 * pair + side
                pieces = []
                for slot in range(CAP):
                    first = table[owner * CAP + slot] * stride + LAG
                    for unit in ORDER:
                        start = pl.multiple_of(first + units[unit], 8)
                        pieces.append(lined[pl.ds(start, UNIT), :].astype(jnp.bfloat16))
                sides.append(jnp.concatenate(pieces, axis=0))
            pltpu.matmul_push_rhs(
                jnp.concatenate(sides, axis=1), pair // 2 % 2, pair % 2, transpose=True
            )
            pltpu.matmul_acc_lhs(total, turn, load_staged_rhs=pair // 2 % 2)
            dealt = pltpu.matmul_pop(total)
            for side in range(2):
                owner = 2 * pair + side
                for slot in range(CAP):
                    tile = dealt[side * LANES:(side + 1) * LANES, slot * LANES:(slot + 1) * LANES]
                    pols = (tile[:LANES // 2], tile[LANES // 2:])
                    moved = pltpu.roll(pick(HALF, pols[1]), 2 * UNIT, 1)
                    value = jnp.concatenate(
                        [
                            pick(WHOLE, pols[0]),
                            jnp.where(shared, pick(HALF, pols[0]), moved),
                            pick(WHOLE, pols[1]),
                        ],
                        axis=1,
                    )
                    target = (owner // columns * CAP + slot) * columns + owner % columns
                    out_ref[target] = value.astype(jnp.bfloat16)

    pl.run_scoped(
        deal, *(pltpu.ACC(mxu_id=index % 2)((2 * LANES, MXU), jnp.float32) for index in range(4))
    )


def spectra(segments, volts, taps, owner_map, owners, columns):
    channels = owner_map.shape[0]
    inputs = volts.shape[1]
    rows = volts.shape[3] // NFFT
    count = sum(segment[2] for segment in segments)
    blocks = sum(-(-(segment[2] + TAPS - 1) // BLOCK) for segment in segments)
    halves = 2 * channels
    stride = 2 * blocks + LAG
    stride = -(-stride // 8) * 8
    trig = jnp.asarray(trig_table(channels))
    hbm = pl.BlockSpec(memory_space=pltpu.HBM)
    return pl.pallas_call(
        functools.partial(spectra_kernel, segments, channels, owners, columns, inputs, rows),
        out_shape=jax.ShapeDtypeStruct((owners * CAP, inputs // 2, 4 * count), jnp.bfloat16),
        in_specs=[hbm] * 4,
        out_specs=pl.BlockSpec(memory_space=pltpu.VMEM),
        scratch_shapes=[
            pltpu.VMEM((blocks, inputs * 2, BLOCK * NFFT), jnp.bfloat16),
            pltpu.VMEM((TAPS * halves, 2 * NFFT), jnp.bfloat16),
            pltpu.VMEM((2 * blocks + LAG, TAPS * halves, LANES), jnp.float32),
            pltpu.VMEM((channels * stride, LANES), jnp.float32),
            pltpu.VMEM(taps.shape, jnp.float32),
            pltpu.VMEM(trig.shape, jnp.float32),
            pltpu.SMEM((channels,), jnp.int32),
            pltpu.SMEM((owners,), jnp.int32),
            pltpu.SMEM((owners * CAP + 1,), jnp.int32),
            pltpu.SemaphoreType.DMA((blocks,)),
            pltpu.SemaphoreType.DMA((3,)),
        ],
        compiler_params=pltpu.CompilerParams(vmem_limit_bytes=48 * 1024 * 1024),
        cost_estimate=pl.CostEstimate(
            flops=4 * blocks * BLOCK * inputs * 2 * NFFT * TAPS * halves,
            bytes_accessed=blocks * BLOCK * inputs * 4 * NFFT, transcendentals=0
        ),
        name="spectra",
    )(*(pltpu.with_memory_space_constraint(x, pltpu.HBM) for x in (owner_map, volts, taps, trig)))


def order_kernel(place_ref, got_ref, cols_ref):
    half = got_ref.shape[0]
    total = 2 * half
    second = pltpu.roll(
        got_ref[:, LANES:2 * LANES].astype(jnp.float32), LANES - 2 * UNIT, 1
    ).astype(jnp.bfloat16)

    def run(*totals):
        for k in range(total // MXU):
            at = slice(k * MXU % half, k * MXU % half + MXU)
            if k * MXU < half:
                right = got_ref[at, :2 * LANES]
            else:
                right = jnp.concatenate([got_ref[at, 2 * LANES:], second[at]], axis=1)
            for unit in range(2):
                pltpu.matmul_push_rhs(right, k % 2, unit)
                pltpu.matmul_acc_lhs(
                    totals[unit],
                    place_ref[unit * half:(unit + 1) * half, k * MXU:(k + 1) * MXU],
                    load_staged_rhs=k % 2,
                )
        for unit in range(2):
            cols_ref[unit * half:(unit + 1) * half] = pltpu.matmul_pop(totals[unit]).astype(
                jnp.bfloat16
            )

    pl.run_scoped(run, *(pltpu.ACC(mxu_id=unit)((half, MXU), jnp.float32) for unit in range(2)))


def order(place, got):
    half = got.shape[0]
    vmem = pl.BlockSpec(memory_space=pltpu.VMEM)
    return pl.pallas_call(
        order_kernel,
        out_shape=jax.ShapeDtypeStruct((2 * half, MXU), jnp.bfloat16),
        in_specs=[vmem] * 2,
        out_specs=vmem,
        compiler_params=pltpu.CompilerParams(vmem_limit_bytes=16 * 1024 * 1024),
        cost_estimate=pl.CostEstimate(
            flops=8 * half * half * MXU, bytes_accessed=8 * half * half, transcendentals=0
        ),
        name="order",
    )(place, got)


def visibility_kernel(scale, mine, row_count, owner_ref, cols_a, cols_b, *rest):
    total = cols_a.shape[0]
    steps = total // MXU
    if mine:
        far, made, near, lead_a, lead_b, sem = rest
        bring = pltpu.make_async_copy(far, near, sem.at[0])
        bring.start()
    else:
        ready, out_hbm, made, lead_a, lead_b, sem = rest
    my_row = lax.axis_index("row")
    slot = my_row if mine else 1 - my_row

    def copy(source, target, step, number):
        return pltpu.make_async_copy(
            source.at[step], out_hbm.at[target, :, :, step * MXU:(step + 1) * MXU], sem.at[number]
        )

    if not mine:
        for step in range(steps):
            copy(ready, my_row, step, step).start()

    first = pl.multiple_of(my_row * row_count, row_count)
    lane = lax.broadcasted_iota(jnp.int32, (row_count, LANES), 1)
    front = lane < LANES // 2
    shared = lane % (LANES // 2) < 2 * UNIT

    for cols, lead in ((cols_a, lead_a), (cols_b, lead_b)):
        for t in range(MXU // LANES):
            at = slice(t * LANES, (t + 1) * LANES)
            own = cols[pl.ds(first, row_count), at].astype(jnp.float32)
            if t == 1:
                own = jnp.where(shared, own, 0.0)
            turned = pltpu.roll(own, LANES // 2, 1)
            lead[0, :, at] = own.astype(jnp.bfloat16)
            lead[1, :, at] = jnp.where(front, turned, -turned).astype(jnp.bfloat16)

    me = lax.axis_index("chan") * lax.axis_size("col") + lax.axis_index("col")
    owned = jnp.int32(0)
    for k in range(owner_ref.shape[0]):
        owned = owned + jnp.where(owner_ref[k] == me, 1, 0)
    factor = jnp.where(slot < owned, jnp.float32(scale), jnp.float32(0.0))

    def run(*totals):
        def flush(step):
            for unit in range(2):
                value = pltpu.matmul_pop(totals[2 * unit + step % 2]) * factor
                made[step, unit] = value.astype(jnp.bfloat16)
            if not mine:
                copy(made, slot, step, steps + step).start()

        for step in range(steps):
            for turn, (cols, lead) in enumerate(((cols_a, lead_a), (cols_b, lead_b))):
                for unit in range(2):
                    pltpu.matmul_push_rhs(
                        cols[step * MXU:(step + 1) * MXU, :], turn, unit, transpose=True
                    )
                    pltpu.matmul_acc_lhs(
                        totals[2 * unit + step % 2], lead[unit], load_staged_rhs=turn
                    )
            if step > 0:
                flush(step - 1)
        flush(steps - 1)

    shape = (row_count, MXU)
    pl.run_scoped(run, *(pltpu.ACC(mxu_id=index // 2)(shape, jnp.float32) for index in range(4)))
    if mine:
        bring.wait()
    else:
        for step in range(steps):
            copy(ready, my_row, step, step).wait()
            copy(made, slot, step, steps + step).wait()


def visibility(scale, owner_map, cols_a, cols_b, row_count, far=None, ready=None):
    total, width = cols_a.shape
    steps = total // MXU
    vmem = pl.BlockSpec(memory_space=pltpu.VMEM)
    hbm = pl.BlockSpec(memory_space=pltpu.HBM)
    kept = (steps, 2, row_count, MXU)
    scratch = [pltpu.VMEM((2, row_count, MXU), jnp.bfloat16)] * 2
    scratch.append(pltpu.SemaphoreType.DMA((2 * steps,)))
    if ready is None:
        more, more_spec = (far,), [hbm]
        out_shape = [jax.ShapeDtypeStruct(shape, jnp.bfloat16) for shape in (kept, (total, width))]
        out_specs = [vmem, vmem]
    else:
        more, more_spec = (ready,), [vmem]
        out_shape = jax.ShapeDtypeStruct((CAP, 2, row_count, total), jnp.bfloat16)
        out_specs = hbm
        scratch.insert(0, pltpu.VMEM(kept, jnp.bfloat16))
    return pl.pallas_call(
        functools.partial(visibility_kernel, scale, ready is None, row_count),
        out_shape=out_shape,
        in_specs=[pl.BlockSpec(memory_space=pltpu.SMEM), vmem, vmem, *more_spec],
        out_specs=out_specs,
        scratch_shapes=scratch,
        compiler_params=pltpu.CompilerParams(vmem_limit_bytes=24 * 1024 * 1024),
        cost_estimate=pl.CostEstimate(
            flops=8 * row_count * total * MXU, bytes_accessed=8 * row_count * total,
            transcendentals=0,
        ),
        name="visibility",
    )(owner_map, cols_a, cols_b, *more)


def tiled_shards(volts, taps, owner_map, assign):
    chan_count = lax.axis_size("chan")
    rows_count = lax.axis_size("row")
    cols_count = lax.axis_size("col")
    owners = chan_count * cols_count
    spec_len = volts.shape[3] // NFFT - TAPS + 1
    total_inputs = 2 * STATIONS
    row_count = total_inputs // rows_count
    positions = jnp.arange(total_inputs, dtype=jnp.int32)
    wanted = positions % 2 * STATIONS + jnp.repeat(assign, 2)
    place = (wanted[:, None] == positions[None, :]).astype(jnp.bfloat16)
    swap = [(0, 1), (1, 0)]
    scale = 1.0 / math.sqrt(2 * BATCHES * spec_len)
    own = []
    other = []
    owner_now = owner_map
    for batch in range(2):
        chunk = ((batch, 0, spec_len),)
        sent = spectra(chunk, volts, taps, owner_now, owners, cols_count)
        owner_now, sent = lax.optimization_barrier((owner_now, sent))
        turned = lax.all_to_all(
            sent, ("chan", "row", "col"), split_axis=0, concat_axis=0, tiled=True
        )
        own.append(order(place, turned.reshape(total_inputs // 2, -1)))
        other.append(lax.ppermute(own[-1], "row", swap))
    ready, near = visibility(scale, owner_map, own[0], own[1], row_count, far=other[0])
    return visibility(scale, owner_map, near, other[1], row_count, ready=ready)


def fits(volts, owner_map, mesh):
    rows = volts.shape[3] // NFFT
    return (
        4 * volts.shape[1] == LANES
        and mesh.shape["row"] == CAP == 2
        and rows - TAPS + 1 == 6 * UNIT
        and owner_map.shape[0] % 8 == 0
        and TAPS * 2 * owner_map.shape[0] <= 384
    )


def solution(mesh):
    placed = (P(None, ("chan", "row", "col"), None, None), P(), P(), P())

    def shards(volts, taps, owner_map, assign):
        if fits(volts, owner_map, mesh):
            return tiled_shards(volts, taps, owner_map, assign)
        return general_shards(volts, taps, owner_map, assign)

    return jax.shard_map(
        shards,
        mesh=mesh,
        in_specs=placed,
        out_specs=P(("chan", "col"), None, "row", None),
        check_vma=False,
    )
```

```python
import functools
import math

import jax
import jax.numpy as jnp
import numpy as np
from jax import lax
from jax.experimental import pallas as pl
from jax.experimental.pallas import tpu as pltpu
from jax.sharding import PartitionSpec as P


STATIONS = 512
NFFT = 512
TAPS = 8
BATCHES = 2
CAP = 2
LANES = 128


def slot_table(owner_map, owner_count, slot_count):
    channel_count = owner_map.shape[0]
    ranking = jnp.argsort(owner_map * channel_count + jnp.arange(channel_count, dtype=jnp.int32))
    counts = jnp.sum(
        (owner_map[None, :] == jnp.arange(owner_count, dtype=jnp.int32)[:, None]).astype(jnp.int32),
        axis=1,
    )
    starts = jnp.cumsum(counts) - counts
    slot_index = jnp.arange(slot_count, dtype=jnp.int32)
    position = jnp.clip(starts[:, None] + slot_index[None, :], 0, channel_count - 1)
    channel = jnp.take(ranking, position, axis=0)
    is_live = slot_index[None, :] < counts[:, None]
    return (channel, is_live)


def general_shards(volts, taps, owner_map, assign):
    chan_count = lax.axis_size("chan")
    rows_count = lax.axis_size("row")
    cols_count = lax.axis_size("col")
    owner_count = chan_count * cols_count
    local_inputs = volts.shape[1]
    spec_len = volts.shape[3] // NFFT - TAPS + 1
    channel, is_live = slot_table(owner_map, owner_count, CAP)
    points = jnp.arange(NFFT, dtype=jnp.int32)
    phase = (points[:, None, None] * channel.T[None, :, :] % NFFT).astype(jnp.float32) * (
        2.0 * math.pi / NFFT
    )
    weight_live = is_live.T[None, :, :].astype(jnp.float32) / math.sqrt(NFFT)
    cosine = jnp.cos(phase) * weight_live
    sine = jnp.sin(phase) * weight_live
    table = jnp.stack(
        [jnp.stack([cosine, -sine], axis=1), jnp.stack([sine, cosine], axis=1)], axis=0
    )
    total_inputs = 2 * STATIONS
    positions = jnp.arange(total_inputs, dtype=jnp.int32)
    pick = 2 * jnp.take(assign, positions // 2, axis=0) + positions % 2
    device_of = pick // local_inputs
    within = pick % local_inputs
    chan_of = device_of // (rows_count * cols_count)
    row_of = device_of // cols_count % rows_count
    col_of = device_of % cols_count
    located = ((row_of * cols_count + col_of) * chan_count + chan_of) * local_inputs + within
    row_count = total_inputs // rows_count
    row_pick = lax.dynamic_slice_in_dim(located, lax.axis_index("row") * row_count, row_count)
    total = jnp.zeros((CAP, 2 * row_count, total_inputs), jnp.float32)
    for batch in range(BATCHES):
        signal = (
            volts[batch].astype(jnp.float32).reshape(local_inputs, 2, spec_len + TAPS - 1, NFFT)
        )
        summed = jnp.zeros((local_inputs, 2, spec_len, NFFT), jnp.float32)
        for tap_index in range(TAPS):
            summed = (
                summed
                + taps[tap_index][None, None, None, :]
                * signal[:, :, tap_index : tap_index + spec_len, :]
            )
        result = jnp.einsum("iasj,ajbkg->kgibs", summed, table, precision=lax.Precision.HIGHEST)
        turned = lax.all_to_all(
            lax.all_to_all(
                result.reshape(CAP, chan_count, cols_count, local_inputs, 2 * spec_len).astype(
                    jnp.bfloat16
                ),
                "chan",
                split_axis=1,
                concat_axis=3,
                tiled=True,
            ),
            "col",
            split_axis=2,
            concat_axis=3,
            tiled=True,
        )
        gathered = lax.all_gather(turned, "row", axis=3, tiled=True)
        flat = gathered.reshape(CAP, total_inputs, -1)
        width = flat.shape[2]
        rows = jnp.take(flat, row_pick, axis=1)
        split_rows = rows.reshape(CAP, row_count, width // (2 * spec_len), 2, spec_len)
        flipped = jnp.stack(
            [split_rows[:, :, :, 1, :], -split_rows[:, :, :, 0, :]], axis=3
        ).reshape(CAP, row_count, width)
        stacked = jnp.concatenate([rows, flipped], axis=1)
        columns = jnp.take(flat, located, axis=1)
        total = total + jnp.einsum(
            "kpx,kqx->kpq", stacked, columns, preferred_element_type=jnp.float32
        )
    scale = 1.0 / math.sqrt(2 * BATCHES * spec_len)
    return (total * scale).reshape(CAP, 2, row_count, total_inputs).astype(jnp.bfloat16)


def trig_table(channels):
    points = np.arange(NFFT)
    phase = (np.arange(channels)[:, None] * points[None, :] % NFFT) * (2.0 * math.pi / NFFT)
    unit = 1.0 / math.sqrt(NFFT)
    return np.concatenate([np.cos(phase), np.sin(phase)], axis=0).astype(np.float32) * np.float32(unit)


BLOCK = 4
MXU = 256
UNROLL = 2
UNIT = 16
ORDER = (0, 1, 2, 2, 0, 1, 2, 2)
WHOLE = ((0, (0, 1, 2)), (1, (3,)), (2, (4, 5, 6)), (3, (7,)))
HALF = ((1, (0, 1)), (3, (4, 5)))
LAG = 8


def spectra_kernel(segments, channels, owners, columns, inputs, rows,
                   owner_hbm, volts_ref, taps_hbm, trig_hbm, out_ref,
                   wave, weight, prod, lined, turn_ref, taps_ref, trig_ref,
                   owner_ref, count, table, made, sem, small, gone):
    blocks = wave.shape[0]
    sets = blocks // UNROLL
    rounds = (sets - 3) // 2
    halves = 2 * channels
    stride = lined.shape[0] // channels
    lanes = 2 * inputs

    loads = [
        pltpu.make_async_copy(taps_hbm, taps_ref, small.at[0]),
        pltpu.make_async_copy(trig_hbm, trig_ref, small.at[1]),
        pltpu.make_async_copy(owner_hbm, owner_ref, small.at[2]),
    ]
    for load in loads:
        load.start()

    units = []
    fetches = []
    for batch, first_row, spectra_count in segments:
        source = volts_ref.at[batch].reshape(lanes, volts_ref.shape[3])
        for u in range(spectra_count // (2 * UNIT)):
            units.append(2 * len(fetches) + u * UNIT)
        for block in range(-(-(spectra_count + TAPS - 1) // BLOCK)):
            fetches.append((source, first_row + block * BLOCK))

    def fetch(block):
        source, row = fetches[block]
        whole = min(BLOCK, rows - row)
        pieces = [(0, row, whole)] + [(step, rows - 1, 1) for step in range(whole, BLOCK)]
        for step, start, held in pieces:
            pltpu.make_async_copy(
                source.at[:, start * NFFT:(start + held) * NFFT],
                wave.at[block, :, step * NFFT:(step + held) * NFFT],
                sem.at[block],
            ).start()

    for block in range(blocks):
        fetch(block)

    stations = inputs // 2
    to = lax.broadcasted_iota(jnp.int32, (2 * LANES, MXU), 0)
    at = lax.broadcasted_iota(jnp.int32, (2 * LANES, MXU), 1)
    row = to % LANES
    quarter = row // stations % 4
    origin = (
        quarter % 2 * lanes + (row % stations * 2 + row // (4 * stations)) * 2 + quarter // 2
        + to - row
    )
    turn_ref[...] = (at == origin).astype(jnp.bfloat16)

    for load in loads:
        load.wait()

    for tap in range(TAPS):
        scaled = trig_ref[...] * taps_ref[tap:tap + 1, :]
        high = scaled.astype(jnp.bfloat16)
        low = (scaled - high.astype(jnp.float32)).astype(jnp.bfloat16)
        weight[tap * halves:(tap + 1) * halves, :NFFT] = high
        weight[tap * halves:(tap + 1) * halves, NFFT:] = low

    for owner in range(owners):
        count[owner] = 0
        for slot in range(CAP):
            table[owner * CAP + slot] = 0
    table[owners * CAP] = 0

    lane = lax.broadcasted_iota(jnp.int32, (halves, LANES), 1)
    low_half = lane < LANES // 2
    even = (lax.broadcasted_iota(jnp.int32, (channels, LANES), 1) % 2) == 0

    def tap_sum(tile, odd):
        total = prod[tile, odd * halves:(odd + 1) * halves, :]
        for e in range(1, TAPS // 2):
            m = 2 * e + odd
            total = total + prod[tile + e, m * halves:(m + 1) * halves, :]
        return total

    def finish(pair, turned):
        for step in range(2 * UNROLL):
            tile = pair + step
            following = pltpu.roll(tap_sum(tile + 1, 1), LANES // 2, 1)
            value = tap_sum(tile, 0) + jnp.where(low_half, turned, following)
            turned = following
            cosine = value[:channels]
            sine = value[channels:]
            mixed = cosine + jnp.where(
                even, pltpu.roll(sine, LANES - 1, 1), -pltpu.roll(sine, 1, 1)
            )
            lined[pl.ds(tile, channels, stride=stride), :] = mixed
        return turned

    def place(k):
        real = k < channels
        owner = owner_ref[jnp.minimum(k, channels - 1)]
        used = count[owner]
        table[jnp.where(real, owner * CAP + used, owners * CAP)] = k
        count[owner] = jnp.where(real, used + 1, used)

    def wait(first):
        for step in range(UNROLL):
            pltpu.make_async_copy(wave.at[first + step], wave.at[first + step], sem.at[first + step]).wait()

    def stage(first, part):
        for step in range(UNROLL):
            x = [
                wave[first + step, :, row * NFFT + part * MXU:row * NFFT + (part + 1) * MXU]
                for row in range(BLOCK)
            ]
            pltpu.matmul_push_rhs(jnp.concatenate(x, axis=0), part, step, transpose=True)

    def multiply(totals, following):
        for part in range(NFFT // MXU):
            for total in totals:
                pltpu.matmul_acc_lhs(
                    total, weight[:, part * MXU:(part + 1) * MXU], load_staged_rhs=part
                )
            if following is not None:
                stage(following, part)
            for total in totals:
                pltpu.matmul_acc_lhs(
                    total, weight[:, NFFT + part * MXU:NFFT + (part + 1) * MXU]
                )

    def collect(first, totals):
        for step, total in enumerate(totals):
            y = pltpu.matmul_pop(total)
            prod[2 * (first + step) + LAG] = y[:, :LANES]
            prod[2 * (first + step) + LAG + 1] = y[:, LANES:]

    def run(*totals):
        even_totals = totals[:2]
        odd_totals = totals[2:]

        share = pl.cdiv(channels, rounds)

        def body(group, turned):
            first = group * 2 * UNROLL
            wait(first + 2 * UNROLL)
            wait(first + 3 * UNROLL)
            for extra in range(share):
                place(group * share + extra)
            multiply(odd_totals, first + 2 * UNROLL)
            turned = finish(2 * first + LAG - 4 - 2 * UNROLL, turned)
            collect(first, even_totals)
            multiply(even_totals, first + 3 * UNROLL)
            turned = finish(2 * first + LAG - 4, turned)
            collect(first + UNROLL, odd_totals)
            return turned

        wait(0)
        wait(UNROLL)
        for part in range(NFFT // MXU):
            stage(0, part)
        multiply(even_totals, UNROLL)
        turned = lax.fori_loop(0, rounds, body, jnp.zeros((halves, LANES), jnp.float32))
        for index in range(2 * rounds + 1, sets):
            if index + 1 < sets:
                wait((index + 1) * UNROLL)
            multiply(
                (even_totals, odd_totals)[index % 2],
                (index + 1) * UNROLL if index + 1 < sets else None,
            )
            turned = finish(4 * (index - 1) + LAG - 8, turned)
            collect((index - 1) * UNROLL, (even_totals, odd_totals)[1 - index % 2])
        turned = finish(4 * (sets - 1) + LAG - 8, turned)
        collect((sets - 1) * UNROLL, (even_totals, odd_totals)[(sets - 1) % 2])
        finish(4 * sets + LAG - 8, turned)

    shape = (TAPS * halves, MXU)
    pl.run_scoped(run, *(pltpu.ACC(mxu_id=index % 2)(shape, jnp.float32) for index in range(4)))

    spot = lax.broadcasted_iota(jnp.int32, (stations, LANES), 1) // UNIT
    shared = spot % 4 < 2

    def pick(choices, dealt):
        value = None
        for quarter, spots in choices:
            piece = dealt[quarter * stations:(quarter + 1) * stations]
            if value is None:
                value = piece
            else:
                inside = functools.reduce(jnp.logical_or, [spot == u for u in spots])
                value = jnp.where(inside, piece, value)
        return value

    def leave(pair):
        ends = pl.ds(pair * 2 * CAP, 2 * CAP)
        return pltpu.make_async_copy(made.at[ends], out_ref.at[ends], gone.at[pair])

    def deal(*totals):
        for pair in range(owners // 2):
            total = totals[pair % len(totals)]
            sides = []
            for side in range(2):
                owner = 2 * pair + side
                pieces = []
                for slot in range(CAP):
                    first = table[owner * CAP + slot] * stride + LAG
                    for unit in ORDER:
                        start = pl.multiple_of(first + units[unit], 8)
                        pieces.append(lined[pl.ds(start, UNIT), :].astype(jnp.bfloat16))
                sides.append(jnp.concatenate(pieces, axis=0))
            pltpu.matmul_push_rhs(
                jnp.concatenate(sides, axis=1), pair // 2 % 2, pair % 2, transpose=True
            )
            pltpu.matmul_acc_lhs(total, turn_ref[...], load_staged_rhs=pair // 2 % 2)
            dealt = pltpu.matmul_pop(total)
            for side in range(2):
                owner = 2 * pair + side
                for slot in range(CAP):
                    tile = dealt[side * LANES:(side + 1) * LANES, slot * LANES:(slot + 1) * LANES]
                    pols = (tile[:LANES // 2], tile[LANES // 2:])
                    moved = pltpu.roll(pick(HALF, pols[1]), 2 * UNIT, 1)
                    value = jnp.concatenate(
                        [
                            pick(WHOLE, pols[0]),
                            jnp.where(shared, pick(HALF, pols[0]), moved),
                            pick(WHOLE, pols[1]),
                        ],
                        axis=1,
                    )
                    target = (owner // columns * CAP + slot) * columns + owner % columns
                    made[target] = value.astype(jnp.bfloat16)
            leave(pair).start()

    pl.run_scoped(
        deal, *(pltpu.ACC(mxu_id=index % 2)((2 * LANES, MXU), jnp.float32) for index in range(4))
    )
    for pair in range(owners // 2):
        leave(pair).wait()


def spectra(segments, volts, taps, owner_map, owners, columns):
    channels = owner_map.shape[0]
    inputs = volts.shape[1]
    rows = volts.shape[3] // NFFT
    count = sum(segment[2] for segment in segments)
    blocks = sum(-(-(segment[2] + TAPS - 1) // BLOCK) for segment in segments)
    halves = 2 * channels
    stride = 2 * blocks + LAG
    stride = -(-stride // 8) * 8
    trig = jnp.asarray(trig_table(channels))
    hbm = pl.BlockSpec(memory_space=pltpu.HBM)
    return pl.pallas_call(
        functools.partial(spectra_kernel, segments, channels, owners, columns, inputs, rows),
        out_shape=jax.ShapeDtypeStruct((owners * CAP, inputs // 2, 4 * count), jnp.bfloat16),
        in_specs=[hbm] * 4,
        out_specs=hbm,
        scratch_shapes=[
            pltpu.VMEM((blocks, inputs * 2, BLOCK * NFFT), jnp.bfloat16),
            pltpu.VMEM((TAPS * halves, 2 * NFFT), jnp.bfloat16),
            pltpu.VMEM((2 * blocks + LAG, TAPS * halves, LANES), jnp.float32),
            pltpu.VMEM((channels * stride, LANES), jnp.float32),
            pltpu.VMEM((2 * LANES, MXU), jnp.bfloat16),
            pltpu.VMEM(taps.shape, jnp.float32),
            pltpu.VMEM(trig.shape, jnp.float32),
            pltpu.SMEM((channels,), jnp.int32),
            pltpu.SMEM((owners,), jnp.int32),
            pltpu.SMEM((owners * CAP + 1,), jnp.int32),
            pltpu.VMEM((owners * CAP, inputs // 2, 4 * count), jnp.bfloat16),
            pltpu.SemaphoreType.DMA((blocks,)),
            pltpu.SemaphoreType.DMA((3,)),
            pltpu.SemaphoreType.DMA((owners // 2,)),
        ],
        compiler_params=pltpu.CompilerParams(vmem_limit_bytes=48 * 1024 * 1024),
        cost_estimate=pl.CostEstimate(
            flops=4 * blocks * BLOCK * inputs * 2 * NFFT * TAPS * halves,
            bytes_accessed=blocks * BLOCK * inputs * 4 * NFFT, transcendentals=0
        ),
        name="spectra",
    )(*(pltpu.with_memory_space_constraint(x, pltpu.HBM) for x in (owner_map, volts, taps, trig)))


def order_kernel(place_ref, got_ref, cols_ref):
    half = got_ref.shape[0]
    total = 2 * half
    second = pltpu.roll(
        got_ref[:, LANES:2 * LANES].astype(jnp.float32), LANES - 2 * UNIT, 1
    ).astype(jnp.bfloat16)

    def run(*totals):
        for k in range(total // MXU):
            at = slice(k * MXU % half, k * MXU % half + MXU)
            if k * MXU < half:
                right = got_ref[at, :2 * LANES]
            else:
                right = jnp.concatenate([got_ref[at, 2 * LANES:], second[at]], axis=1)
            for unit in range(2):
                pltpu.matmul_push_rhs(right, k % 2, unit)
                pltpu.matmul_acc_lhs(
                    totals[unit],
                    place_ref[unit * half:(unit + 1) * half, k * MXU:(k + 1) * MXU],
                    load_staged_rhs=k % 2,
                )
        for unit in range(2):
            cols_ref[unit * half:(unit + 1) * half] = pltpu.matmul_pop(totals[unit]).astype(
                jnp.bfloat16
            )

    pl.run_scoped(run, *(pltpu.ACC(mxu_id=unit)((half, MXU), jnp.float32) for unit in range(2)))


def order(place, got):
    half = got.shape[0]
    vmem = pl.BlockSpec(memory_space=pltpu.VMEM)
    return pl.pallas_call(
        order_kernel,
        out_shape=jax.ShapeDtypeStruct((2 * half, MXU), jnp.bfloat16),
        in_specs=[vmem] * 2,
        out_specs=vmem,
        compiler_params=pltpu.CompilerParams(vmem_limit_bytes=16 * 1024 * 1024),
        cost_estimate=pl.CostEstimate(
            flops=8 * half * half * MXU, bytes_accessed=8 * half * half, transcendentals=0
        ),
        name="order",
    )(place, got)


def visibility_kernel(scale, mine, row_count, owner_ref, cols_a, cols_b, *rest):
    total = cols_a.shape[0]
    steps = total // MXU
    if mine:
        far, made, near, lead_a, lead_b, sem = rest
        bring = pltpu.make_async_copy(far, near, sem.at[0])
        bring.start()
    else:
        ready, out_hbm, made, lead_a, lead_b, sem = rest
    my_row = lax.axis_index("row")
    slot = my_row if mine else 1 - my_row

    def copy(source, target, step, number):
        return pltpu.make_async_copy(
            source.at[step], out_hbm.at[target, :, :, step * MXU:(step + 1) * MXU], sem.at[number]
        )

    def copy_part(step, unit):
        return pltpu.make_async_copy(
            made.at[step, unit],
            out_hbm.at[slot, unit, :, step * MXU:(step + 1) * MXU],
            sem.at[steps + 2 * step + unit],
        )

    if not mine:
        for step in range(steps):
            copy(ready, my_row, step, step).start()

    first = pl.multiple_of(my_row * row_count, row_count)
    lane = lax.broadcasted_iota(jnp.int32, (row_count, LANES), 1)
    front = lane < LANES // 2
    shared = lane % (LANES // 2) < 2 * UNIT

    for cols, lead in ((cols_a, lead_a), (cols_b, lead_b)):
        for t in range(MXU // LANES):
            at = slice(t * LANES, (t + 1) * LANES)
            own = cols[pl.ds(first, row_count), at].astype(jnp.float32)
            if t == 1:
                own = jnp.where(shared, own, 0.0)
            turned = pltpu.roll(own, LANES // 2, 1)
            lead[0, :, at] = own.astype(jnp.bfloat16)
            lead[1, :, at] = jnp.where(front, turned, -turned).astype(jnp.bfloat16)

    me = lax.axis_index("chan") * lax.axis_size("col") + lax.axis_index("col")
    owned = jnp.int32(0)
    for k in range(owner_ref.shape[0]):
        owned = owned + jnp.where(owner_ref[k] == me, 1, 0)
    factor = jnp.where(slot < owned, jnp.float32(scale), jnp.float32(0.0))

    def run(*totals):
        def flush(step):
            for unit in range(2):
                value = pltpu.matmul_pop(totals[2 * unit + step % 2]) * factor
                made[step, unit] = value.astype(jnp.bfloat16)
                if not mine:
                    copy_part(step, unit).start()

        for step in range(steps):
            for turn, (cols, lead) in enumerate(((cols_a, lead_a), (cols_b, lead_b))):
                for unit in range(2):
                    pltpu.matmul_push_rhs(
                        cols[step * MXU:(step + 1) * MXU, :], turn, unit, transpose=True
                    )
                    pltpu.matmul_acc_lhs(
                        totals[2 * unit + step % 2], lead[unit], load_staged_rhs=turn
                    )
            if step > 0:
                flush(step - 1)
        flush(steps - 1)

    shape = (row_count, MXU)
    pl.run_scoped(run, *(pltpu.ACC(mxu_id=index // 2)(shape, jnp.float32) for index in range(4)))
    if mine:
        bring.wait()
    else:
        for step in range(steps):
            copy(ready, my_row, step, step).wait()
            for unit in range(2):
                copy_part(step, unit).wait()


def visibility(scale, owner_map, cols_a, cols_b, row_count, far=None, ready=None):
    total, width = cols_a.shape
    steps = total // MXU
    vmem = pl.BlockSpec(memory_space=pltpu.VMEM)
    hbm = pl.BlockSpec(memory_space=pltpu.HBM)
    kept = (steps, 2, row_count, MXU)
    scratch = [pltpu.VMEM((2, row_count, MXU), jnp.bfloat16)] * 2
    scratch.append(pltpu.SemaphoreType.DMA((3 * steps,)))
    if ready is None:
        more, more_spec = (far,), [hbm]
        out_shape = [jax.ShapeDtypeStruct(shape, jnp.bfloat16) for shape in (kept, (total, width))]
        out_specs = [vmem, vmem]
    else:
        more, more_spec = (ready,), [vmem]
        out_shape = jax.ShapeDtypeStruct((CAP, 2, row_count, total), jnp.bfloat16)
        out_specs = hbm
        scratch.insert(0, pltpu.VMEM(kept, jnp.bfloat16))
    return pl.pallas_call(
        functools.partial(visibility_kernel, scale, ready is None, row_count),
        out_shape=out_shape,
        in_specs=[pl.BlockSpec(memory_space=pltpu.SMEM), vmem, vmem, *more_spec],
        out_specs=out_specs,
        scratch_shapes=scratch,
        compiler_params=pltpu.CompilerParams(vmem_limit_bytes=24 * 1024 * 1024),
        cost_estimate=pl.CostEstimate(
            flops=8 * row_count * total * MXU, bytes_accessed=8 * row_count * total,
            transcendentals=0,
        ),
        name="visibility",
    )(owner_map, cols_a, cols_b, *more)


def tiled_shards(volts, taps, owner_map, assign):
    chan_count = lax.axis_size("chan")
    rows_count = lax.axis_size("row")
    cols_count = lax.axis_size("col")
    owners = chan_count * cols_count
    spec_len = volts.shape[3] // NFFT - TAPS + 1
    total_inputs = 2 * STATIONS
    row_count = total_inputs // rows_count
    positions = jnp.arange(total_inputs, dtype=jnp.int32)
    wanted = positions % 2 * STATIONS + jnp.repeat(assign, 2)
    place = (wanted[:, None] == positions[None, :]).astype(jnp.bfloat16)
    swap = [(0, 1), (1, 0)]
    scale = 1.0 / math.sqrt(2 * BATCHES * spec_len)
    own = []
    other = []
    owner_now = owner_map
    for batch in range(2):
        chunk = ((batch, 0, spec_len),)
        sent = spectra(chunk, volts, taps, owner_now, owners, cols_count)
        owner_now, sent = lax.optimization_barrier((owner_now, sent))
        turned = lax.all_to_all(
            sent, ("chan", "row", "col"), split_axis=0, concat_axis=0, tiled=True
        )
        own.append(order(place, turned.reshape(total_inputs // 2, -1)))
        other.append(lax.ppermute(own[-1], "row", swap))
    ready, near = visibility(scale, owner_map, own[0], own[1], row_count, far=other[0])
    return visibility(scale, owner_map, near, other[1], row_count, ready=ready)


def fits(volts, owner_map, mesh):
    rows = volts.shape[3] // NFFT
    return (
        4 * volts.shape[1] == LANES
        and mesh.shape["row"] == mesh.shape["col"] == CAP == 2
        and rows - TAPS + 1 == 6 * UNIT
        and owner_map.shape[0] % 8 == 0
        and TAPS * 2 * owner_map.shape[0] <= 384
    )


def solution(mesh):
    placed = (P(None, ("chan", "row", "col"), None, None), P(), P(), P())

    def shards(volts, taps, owner_map, assign):
        if fits(volts, owner_map, mesh):
            return tiled_shards(volts, taps, owner_map, assign)
        return general_shards(volts, taps, owner_map, assign)

    return jax.shard_map(
        shards,
        mesh=mesh,
        in_specs=placed,
        out_specs=P(("chan", "col"), None, "row", None),
        check_vma=False,
    )
```

```python
import functools
import math

import jax
import jax.numpy as jnp
import numpy as np
from jax import lax
from jax.experimental import pallas as pl
from jax.experimental.pallas import tpu as pltpu
from jax.sharding import PartitionSpec as P


STATIONS = 512
NFFT = 512
TAPS = 8
BATCHES = 2
CAP = 2
LANES = 128


def slot_table(owner_map, owner_count, slot_count):
    channel_count = owner_map.shape[0]
    ranking = jnp.argsort(owner_map * channel_count + jnp.arange(channel_count, dtype=jnp.int32))
    counts = jnp.sum(
        (owner_map[None, :] == jnp.arange(owner_count, dtype=jnp.int32)[:, None]).astype(jnp.int32),
        axis=1,
    )
    starts = jnp.cumsum(counts) - counts
    slot_index = jnp.arange(slot_count, dtype=jnp.int32)
    position = jnp.clip(starts[:, None] + slot_index[None, :], 0, channel_count - 1)
    channel = jnp.take(ranking, position, axis=0)
    is_live = slot_index[None, :] < counts[:, None]
    return (channel, is_live)


def general_shards(volts, taps, owner_map, assign):
    chan_count = lax.axis_size("chan")
    rows_count = lax.axis_size("row")
    cols_count = lax.axis_size("col")
    owner_count = chan_count * cols_count
    local_inputs = volts.shape[1]
    spec_len = volts.shape[3] // NFFT - TAPS + 1
    channel, is_live = slot_table(owner_map, owner_count, CAP)
    points = jnp.arange(NFFT, dtype=jnp.int32)
    phase = (points[:, None, None] * channel.T[None, :, :] % NFFT).astype(jnp.float32) * (
        2.0 * math.pi / NFFT
    )
    weight_live = is_live.T[None, :, :].astype(jnp.float32) / math.sqrt(NFFT)
    cosine = jnp.cos(phase) * weight_live
    sine = jnp.sin(phase) * weight_live
    table = jnp.stack(
        [jnp.stack([cosine, -sine], axis=1), jnp.stack([sine, cosine], axis=1)], axis=0
    )
    total_inputs = 2 * STATIONS
    positions = jnp.arange(total_inputs, dtype=jnp.int32)
    pick = 2 * jnp.take(assign, positions // 2, axis=0) + positions % 2
    device_of = pick // local_inputs
    within = pick % local_inputs
    chan_of = device_of // (rows_count * cols_count)
    row_of = device_of // cols_count % rows_count
    col_of = device_of % cols_count
    located = ((row_of * cols_count + col_of) * chan_count + chan_of) * local_inputs + within
    row_count = total_inputs // rows_count
    row_pick = lax.dynamic_slice_in_dim(located, lax.axis_index("row") * row_count, row_count)
    total = jnp.zeros((CAP, 2 * row_count, total_inputs), jnp.float32)
    for batch in range(BATCHES):
        signal = (
            volts[batch].astype(jnp.float32).reshape(local_inputs, 2, spec_len + TAPS - 1, NFFT)
        )
        summed = jnp.zeros((local_inputs, 2, spec_len, NFFT), jnp.float32)
        for tap_index in range(TAPS):
            summed = (
                summed
                + taps[tap_index][None, None, None, :]
                * signal[:, :, tap_index : tap_index + spec_len, :]
            )
        result = jnp.einsum("iasj,ajbkg->kgibs", summed, table, precision=lax.Precision.HIGHEST)
        turned = lax.all_to_all(
            lax.all_to_all(
                result.reshape(CAP, chan_count, cols_count, local_inputs, 2 * spec_len).astype(
                    jnp.bfloat16
                ),
                "chan",
                split_axis=1,
                concat_axis=3,
                tiled=True,
            ),
            "col",
            split_axis=2,
            concat_axis=3,
            tiled=True,
        )
        gathered = lax.all_gather(turned, "row", axis=3, tiled=True)
        flat = gathered.reshape(CAP, total_inputs, -1)
        width = flat.shape[2]
        rows = jnp.take(flat, row_pick, axis=1)
        split_rows = rows.reshape(CAP, row_count, width // (2 * spec_len), 2, spec_len)
        flipped = jnp.stack(
            [split_rows[:, :, :, 1, :], -split_rows[:, :, :, 0, :]], axis=3
        ).reshape(CAP, row_count, width)
        stacked = jnp.concatenate([rows, flipped], axis=1)
        columns = jnp.take(flat, located, axis=1)
        total = total + jnp.einsum(
            "kpx,kqx->kpq", stacked, columns, preferred_element_type=jnp.float32
        )
    scale = 1.0 / math.sqrt(2 * BATCHES * spec_len)
    return (total * scale).reshape(CAP, 2, row_count, total_inputs).astype(jnp.bfloat16)


def trig_table(channels):
    points = np.arange(NFFT)
    phase = (np.arange(channels)[:, None] * points[None, :] % NFFT) * (2.0 * math.pi / NFFT)
    unit = 1.0 / math.sqrt(NFFT)
    return np.concatenate([np.cos(phase), np.sin(phase)], axis=0).astype(np.float32) * np.float32(unit)


BLOCK = 4
MXU = 256
UNROLL = 2
UNIT = 16
ORDER = (0, 1, 2, 2, 0, 1, 2, 2)
WHOLE = ((0, (0, 1, 2)), (1, (3,)), (2, (4, 5, 6)), (3, (7,)))
HALF = ((1, (0, 1)), (3, (4, 5)))
LAG = 8


def spectra_kernel(segments, channels, owners, columns, inputs, rows,
                   owner_hbm, volts_ref, taps_hbm, trig_hbm, out_ref,
                   wave, weight, prod, lined, turn_ref, taps_ref, trig_ref,
                   owner_ref, count, table, made, sem, small, gone):
    blocks = wave.shape[0]
    sets = blocks // UNROLL
    rounds = (sets - 3) // 2
    halves = 2 * channels
    stride = lined.shape[0] // channels
    lanes = 2 * inputs

    loads = [
        pltpu.make_async_copy(taps_hbm, taps_ref, small.at[0]),
        pltpu.make_async_copy(trig_hbm, trig_ref, small.at[1]),
        pltpu.make_async_copy(owner_hbm, owner_ref, small.at[2]),
    ]
    for load in loads:
        load.start()

    units = []
    fetches = []
    for batch, first_row, spectra_count in segments:
        source = volts_ref.at[batch].reshape(lanes, volts_ref.shape[3])
        for u in range(spectra_count // (2 * UNIT)):
            units.append(2 * len(fetches) + u * UNIT)
        for block in range(-(-(spectra_count + TAPS - 1) // BLOCK)):
            fetches.append((source, first_row + block * BLOCK))

    def fetch(block):
        source, row = fetches[block]
        whole = min(BLOCK, rows - row)
        pieces = [(0, row, whole)] + [(step, rows - 1, 1) for step in range(whole, BLOCK)]
        for step, start, held in pieces:
            pltpu.make_async_copy(
                source.at[:, start * NFFT:(start + held) * NFFT],
                wave.at[block, :, step * NFFT:(step + held) * NFFT],
                sem.at[block],
            ).start()

    for block in range(blocks):
        fetch(block)

    stations = inputs // 2
    to = lax.broadcasted_iota(jnp.int32, (2 * LANES, MXU), 0)
    at = lax.broadcasted_iota(jnp.int32, (2 * LANES, MXU), 1)
    row = to % LANES
    quarter = row // stations % 4
    origin = (
        quarter % 2 * lanes + (row % stations * 2 + row // (4 * stations)) * 2 + quarter // 2
        + to - row
    )
    turn_ref[...] = (at == origin).astype(jnp.bfloat16)

    for load in loads:
        load.wait()

    for tap in range(TAPS):
        scaled = trig_ref[...] * taps_ref[tap:tap + 1, :]
        high = scaled.astype(jnp.bfloat16)
        low = (scaled - high.astype(jnp.float32)).astype(jnp.bfloat16)
        weight[tap * halves:(tap + 1) * halves, :NFFT] = high
        weight[tap * halves:(tap + 1) * halves, NFFT:] = low

    for owner in range(owners):
        count[owner] = 0
        for slot in range(CAP):
            table[owner * CAP + slot] = 0
    table[owners * CAP] = 0

    lane = lax.broadcasted_iota(jnp.int32, (halves, LANES), 1)
    low_half = lane < LANES // 2
    even = (lax.broadcasted_iota(jnp.int32, (channels, LANES), 1) % 2) == 0

    def tap_sum(tile, odd):
        total = prod[tile, odd * halves:(odd + 1) * halves, :]
        for e in range(1, TAPS // 2):
            m = 2 * e + odd
            total = total + prod[tile + e, m * halves:(m + 1) * halves, :]
        return total

    def finish(pair, turned):
        for step in range(2 * UNROLL):
            tile = pair + step
            following = pltpu.roll(tap_sum(tile + 1, 1), LANES // 2, 1)
            value = tap_sum(tile, 0) + jnp.where(low_half, turned, following)
            turned = following
            cosine = value[:channels]
            sine = value[channels:]
            mixed = cosine + jnp.where(
                even, pltpu.roll(sine, LANES - 1, 1), -pltpu.roll(sine, 1, 1)
            )
            lined[pl.ds(tile, channels, stride=stride), :] = mixed
        return turned

    def place(k):
        real = k < channels
        owner = owner_ref[jnp.minimum(k, channels - 1)]
        used = count[owner]
        table[jnp.where(real, owner * CAP + used, owners * CAP)] = k
        count[owner] = jnp.where(real, used + 1, used)

    def wait(first):
        for step in range(UNROLL):
            pltpu.make_async_copy(wave.at[first + step], wave.at[first + step], sem.at[first + step]).wait()

    def stage(first, part):
        for step in range(UNROLL):
            x = [
                wave[first + step, :, row * NFFT + part * MXU:row * NFFT + (part + 1) * MXU]
                for row in range(BLOCK)
            ]
            pltpu.matmul_push_rhs(jnp.concatenate(x, axis=0), part, step, transpose=True)

    def multiply(totals, following):
        for part in range(NFFT // MXU):
            for total in totals:
                pltpu.matmul_acc_lhs(
                    total, weight[:, part * MXU:(part + 1) * MXU], load_staged_rhs=part
                )
            if following is not None:
                stage(following, part)
            for total in totals:
                pltpu.matmul_acc_lhs(
                    total, weight[:, NFFT + part * MXU:NFFT + (part + 1) * MXU]
                )

    def collect(first, totals):
        for step, total in enumerate(totals):
            y = pltpu.matmul_pop(total)
            prod[2 * (first + step) + LAG] = y[:, :LANES]
            prod[2 * (first + step) + LAG + 1] = y[:, LANES:]

    def run(*totals):
        even_totals = totals[:2]
        odd_totals = totals[2:]

        share = pl.cdiv(channels, rounds)

        def body(group, turned):
            first = group * 2 * UNROLL
            wait(first + 2 * UNROLL)
            wait(first + 3 * UNROLL)
            for extra in range(share):
                place(group * share + extra)
            multiply(odd_totals, first + 2 * UNROLL)
            turned = finish(2 * first + LAG - 4 - 2 * UNROLL, turned)
            collect(first, even_totals)
            multiply(even_totals, first + 3 * UNROLL)
            turned = finish(2 * first + LAG - 4, turned)
            collect(first + UNROLL, odd_totals)
            return turned

        wait(0)
        wait(UNROLL)
        for part in range(NFFT // MXU):
            stage(0, part)
        multiply(even_totals, UNROLL)
        turned = lax.fori_loop(0, rounds, body, jnp.zeros((halves, LANES), jnp.float32))
        for index in range(2 * rounds + 1, sets):
            if index + 1 < sets:
                wait((index + 1) * UNROLL)
            multiply(
                (even_totals, odd_totals)[index % 2],
                (index + 1) * UNROLL if index + 1 < sets else None,
            )
            turned = finish(4 * (index - 1) + LAG - 8, turned)
            collect((index - 1) * UNROLL, (even_totals, odd_totals)[1 - index % 2])
        turned = finish(4 * (sets - 1) + LAG - 8, turned)
        collect((sets - 1) * UNROLL, (even_totals, odd_totals)[(sets - 1) % 2])
        finish(4 * sets + LAG - 8, turned)

    shape = (TAPS * halves, MXU)
    pl.run_scoped(run, *(pltpu.ACC(mxu_id=index % 2)(shape, jnp.float32) for index in range(4)))

    spot = lax.broadcasted_iota(jnp.int32, (stations, LANES), 1) // UNIT
    shared = spot % 4 < 2

    def pick(choices, dealt):
        value = None
        for quarter, spots in choices:
            piece = dealt[quarter * stations:(quarter + 1) * stations]
            if value is None:
                value = piece
            else:
                inside = functools.reduce(jnp.logical_or, [spot == u for u in spots])
                value = jnp.where(inside, piece, value)
        return value

    def leave(pair):
        ends = pl.ds(pair * 2 * CAP, 2 * CAP)
        return pltpu.make_async_copy(made.at[ends], out_ref.at[ends], gone.at[pair])

    def deal(*totals):
        for pair in range(owners // 2):
            total = totals[pair % len(totals)]
            sides = []
            for side in range(2):
                owner = 2 * pair + side
                pieces = []
                for slot in range(CAP):
                    first = table[owner * CAP + slot] * stride + LAG
                    for unit in ORDER:
                        start = pl.multiple_of(first + units[unit], 8)
                        pieces.append(lined[pl.ds(start, UNIT), :].astype(jnp.bfloat16))
                sides.append(jnp.concatenate(pieces, axis=0))
            pltpu.matmul_push_rhs(
                jnp.concatenate(sides, axis=1), pair // 2 % 2, pair % 2, transpose=True
            )
            pltpu.matmul_acc_lhs(total, turn_ref[...], load_staged_rhs=pair // 2 % 2)
            dealt = pltpu.matmul_pop(total)
            for side in range(2):
                owner = 2 * pair + side
                for slot in range(CAP):
                    tile = dealt[side * LANES:(side + 1) * LANES, slot * LANES:(slot + 1) * LANES]
                    pols = (tile[:LANES // 2], tile[LANES // 2:])
                    moved = pltpu.roll(pick(HALF, pols[1]), 2 * UNIT, 1)
                    value = jnp.concatenate(
                        [
                            pick(WHOLE, pols[0]),
                            jnp.where(shared, pick(HALF, pols[0]), moved),
                            pick(WHOLE, pols[1]),
                        ],
                        axis=1,
                    )
                    target = (owner // columns * CAP + slot) * columns + owner % columns
                    made[target] = value.astype(jnp.bfloat16)
            leave(pair).start()

    pl.run_scoped(
        deal, *(pltpu.ACC(mxu_id=index % 2)((2 * LANES, MXU), jnp.float32) for index in range(4))
    )
    for pair in range(owners // 2):
        leave(pair).wait()


def spectra(segments, volts, taps, owner_map, owners, columns):
    channels = owner_map.shape[0]
    inputs = volts.shape[1]
    rows = volts.shape[3] // NFFT
    count = sum(segment[2] for segment in segments)
    blocks = sum(-(-(segment[2] + TAPS - 1) // BLOCK) for segment in segments)
    halves = 2 * channels
    stride = 2 * blocks + LAG
    stride = -(-stride // 8) * 8
    trig = jnp.asarray(trig_table(channels))
    hbm = pl.BlockSpec(memory_space=pltpu.HBM)
    return pl.pallas_call(
        functools.partial(spectra_kernel, segments, channels, owners, columns, inputs, rows),
        out_shape=jax.ShapeDtypeStruct((owners * CAP, inputs // 2, 4 * count), jnp.bfloat16),
        in_specs=[hbm] * 4,
        out_specs=hbm,
        scratch_shapes=[
            pltpu.VMEM((blocks, inputs * 2, BLOCK * NFFT), jnp.bfloat16),
            pltpu.VMEM((TAPS * halves, 2 * NFFT), jnp.bfloat16),
            pltpu.VMEM((2 * blocks + LAG, TAPS * halves, LANES), jnp.float32),
            pltpu.VMEM((channels * stride, LANES), jnp.float32),
            pltpu.VMEM((2 * LANES, MXU), jnp.bfloat16),
            pltpu.VMEM(taps.shape, jnp.float32),
            pltpu.VMEM(trig.shape, jnp.float32),
            pltpu.SMEM((channels,), jnp.int32),
            pltpu.SMEM((owners,), jnp.int32),
            pltpu.SMEM((owners * CAP + 1,), jnp.int32),
            pltpu.VMEM((owners * CAP, inputs // 2, 4 * count), jnp.bfloat16),
            pltpu.SemaphoreType.DMA((blocks,)),
            pltpu.SemaphoreType.DMA((3,)),
            pltpu.SemaphoreType.DMA((owners // 2,)),
        ],
        compiler_params=pltpu.CompilerParams(vmem_limit_bytes=48 * 1024 * 1024),
        cost_estimate=pl.CostEstimate(
            flops=4 * blocks * BLOCK * inputs * 2 * NFFT * TAPS * halves,
            bytes_accessed=blocks * BLOCK * inputs * 4 * NFFT, transcendentals=0
        ),
        name="spectra",
    )(*(pltpu.with_memory_space_constraint(x, pltpu.HBM) for x in (owner_map, volts, taps, trig)))


def order_kernel(place_ref, got_ref, cols_ref):
    half = got_ref.shape[0]
    total = 2 * half
    second = pltpu.roll(
        got_ref[:, LANES:2 * LANES].astype(jnp.float32), LANES - 2 * UNIT, 1
    ).astype(jnp.bfloat16)

    piece = half // 2

    def run(*totals):
        for index in range(2):
            for k in range(total // MXU):
                at = slice(k * MXU % half, k * MXU % half + MXU)
                if k * MXU < half:
                    right = got_ref[at, :2 * LANES]
                else:
                    right = jnp.concatenate([got_ref[at, 2 * LANES:], second[at]], axis=1)
                for unit in range(2):
                    first = unit * half + index * piece
                    pltpu.matmul_push_rhs(right, k % 2, unit)
                    pltpu.matmul_acc_lhs(
                        totals[2 * unit + index],
                        place_ref[first:first + piece, k * MXU:(k + 1) * MXU],
                        load_staged_rhs=k % 2,
                    )
        for index in range(2):
            for unit in range(2):
                first = unit * half + index * piece
                cols_ref[first:first + piece] = pltpu.matmul_pop(
                    totals[2 * unit + index]
                ).astype(jnp.bfloat16)

    pl.run_scoped(
        run, *(pltpu.ACC(mxu_id=index // 2)((piece, MXU), jnp.float32) for index in range(4))
    )


def order(place, got):
    half = got.shape[0]
    vmem = pl.BlockSpec(memory_space=pltpu.VMEM)
    return pl.pallas_call(
        order_kernel,
        out_shape=jax.ShapeDtypeStruct((2 * half, MXU), jnp.bfloat16),
        in_specs=[vmem] * 2,
        out_specs=vmem,
        compiler_params=pltpu.CompilerParams(vmem_limit_bytes=16 * 1024 * 1024),
        cost_estimate=pl.CostEstimate(
            flops=8 * half * half * MXU, bytes_accessed=8 * half * half, transcendentals=0
        ),
        name="order",
    )(place, got)


def visibility_kernel(scale, mine, row_count, owner_ref, cols_a, cols_b, *rest):
    total = cols_a.shape[0]
    steps = total // MXU
    if mine:
        far, made, near, lead_a, lead_b, sem = rest
        bring = pltpu.make_async_copy(far, near, sem.at[0])
        bring.start()
    else:
        ready, out_hbm, made, lead_a, lead_b, sem = rest
    my_row = lax.axis_index("row")
    slot = my_row if mine else 1 - my_row

    def copy(source, target, step, number):
        return pltpu.make_async_copy(
            source.at[step], out_hbm.at[target, :, :, step * MXU:(step + 1) * MXU], sem.at[number]
        )

    def copy_part(step, unit):
        return pltpu.make_async_copy(
            made.at[step, unit],
            out_hbm.at[slot, unit, :, step * MXU:(step + 1) * MXU],
            sem.at[steps + 2 * step + unit],
        )

    if not mine:
        for step in range(steps):
            copy(ready, my_row, step, step).start()

    first = pl.multiple_of(my_row * row_count, row_count)
    lane = lax.broadcasted_iota(jnp.int32, (row_count, LANES), 1)
    front = lane < LANES // 2
    shared = lane % (LANES // 2) < 2 * UNIT

    for cols, lead in ((cols_a, lead_a), (cols_b, lead_b)):
        for t in range(MXU // LANES):
            at = slice(t * LANES, (t + 1) * LANES)
            own = cols[pl.ds(first, row_count), at].astype(jnp.float32)
            if t == 1:
                own = jnp.where(shared, own, 0.0)
            turned = pltpu.roll(own, LANES // 2, 1)
            lead[0, :, at] = own.astype(jnp.bfloat16)
            lead[1, :, at] = jnp.where(front, turned, -turned).astype(jnp.bfloat16)

    me = lax.axis_index("chan") * lax.axis_size("col") + lax.axis_index("col")
    owned = jnp.int32(0)
    for k in range(owner_ref.shape[0]):
        owned = owned + jnp.where(owner_ref[k] == me, 1, 0)
    factor = jnp.where(slot < owned, jnp.float32(scale), jnp.float32(0.0))

    def run(*totals):
        def flush(step):
            for unit in range(2):
                value = pltpu.matmul_pop(totals[2 * unit + step % 2]) * factor
                made[step, unit] = value.astype(jnp.bfloat16)
                if not mine:
                    copy_part(step, unit).start()

        for step in range(steps):
            for turn, (cols, lead) in enumerate(((cols_a, lead_a), (cols_b, lead_b))):
                for unit in range(2):
                    pltpu.matmul_push_rhs(
                        cols[step * MXU:(step + 1) * MXU, :], turn, unit, transpose=True
                    )
                    pltpu.matmul_acc_lhs(
                        totals[2 * unit + step % 2], lead[unit], load_staged_rhs=turn
                    )
            if step > 0:
                flush(step - 1)
        flush(steps - 1)

    shape = (row_count, MXU)
    pl.run_scoped(run, *(pltpu.ACC(mxu_id=index // 2)(shape, jnp.float32) for index in range(4)))
    if mine:
        bring.wait()
    else:
        for step in range(steps):
            copy(ready, my_row, step, step).wait()
            for unit in range(2):
                copy_part(step, unit).wait()


def visibility(scale, owner_map, cols_a, cols_b, row_count, far=None, ready=None):
    total, width = cols_a.shape
    steps = total // MXU
    vmem = pl.BlockSpec(memory_space=pltpu.VMEM)
    hbm = pl.BlockSpec(memory_space=pltpu.HBM)
    kept = (steps, 2, row_count, MXU)
    scratch = [pltpu.VMEM((2, row_count, MXU), jnp.bfloat16)] * 2
    scratch.append(pltpu.SemaphoreType.DMA((3 * steps,)))
    if ready is None:
        more, more_spec = (far,), [hbm]
        out_shape = [jax.ShapeDtypeStruct(shape, jnp.bfloat16) for shape in (kept, (total, width))]
        out_specs = [vmem, vmem]
    else:
        more, more_spec = (ready,), [vmem]
        out_shape = jax.ShapeDtypeStruct((CAP, 2, row_count, total), jnp.bfloat16)
        out_specs = hbm
        scratch.insert(0, pltpu.VMEM(kept, jnp.bfloat16))
    return pl.pallas_call(
        functools.partial(visibility_kernel, scale, ready is None, row_count),
        out_shape=out_shape,
        in_specs=[pl.BlockSpec(memory_space=pltpu.SMEM), vmem, vmem, *more_spec],
        out_specs=out_specs,
        scratch_shapes=scratch,
        compiler_params=pltpu.CompilerParams(vmem_limit_bytes=24 * 1024 * 1024),
        cost_estimate=pl.CostEstimate(
            flops=8 * row_count * total * MXU, bytes_accessed=8 * row_count * total,
            transcendentals=0,
        ),
        name="visibility",
    )(owner_map, cols_a, cols_b, *more)


def tiled_shards(volts, taps, owner_map, assign):
    chan_count = lax.axis_size("chan")
    rows_count = lax.axis_size("row")
    cols_count = lax.axis_size("col")
    owners = chan_count * cols_count
    spec_len = volts.shape[3] // NFFT - TAPS + 1
    total_inputs = 2 * STATIONS
    row_count = total_inputs // rows_count
    positions = jnp.arange(total_inputs, dtype=jnp.int32)
    wanted = positions % 2 * STATIONS + jnp.repeat(assign, 2)
    place = (wanted[:, None] == positions[None, :]).astype(jnp.bfloat16)
    swap = [(0, 1), (1, 0)]
    scale = 1.0 / math.sqrt(2 * BATCHES * spec_len)
    own = []
    other = []
    owner_now = owner_map
    for batch in range(2):
        chunk = ((batch, 0, spec_len),)
        sent = spectra(chunk, volts, taps, owner_now, owners, cols_count)
        owner_now, sent = lax.optimization_barrier((owner_now, sent))
        turned = lax.all_to_all(
            sent, ("chan", "row", "col"), split_axis=0, concat_axis=0, tiled=True
        )
        own.append(order(place, turned.reshape(total_inputs // 2, -1)))
        other.append(lax.ppermute(own[-1], "row", swap))
    ready, near = visibility(scale, owner_map, own[0], own[1], row_count, far=other[0])
    return visibility(scale, owner_map, near, other[1], row_count, ready=ready)


def fits(volts, owner_map, mesh):
    rows = volts.shape[3] // NFFT
    return (
        4 * volts.shape[1] == LANES
        and mesh.shape["row"] == mesh.shape["col"] == CAP == 2
        and rows - TAPS + 1 == 6 * UNIT
        and owner_map.shape[0] % 8 == 0
        and TAPS * 2 * owner_map.shape[0] <= 384
    )


def solution(mesh):
    placed = (P(None, ("chan", "row", "col"), None, None), P(), P(), P())

    def shards(volts, taps, owner_map, assign):
        if fits(volts, owner_map, mesh):
            return tiled_shards(volts, taps, owner_map, assign)
        return general_shards(volts, taps, owner_map, assign)

    return jax.shard_map(
        shards,
        mesh=mesh,
        in_specs=placed,
        out_specs=P(("chan", "col"), None, "row", None),
        check_vma=False,
    )
```
